256 devices in a mesh: leaf: 16 (over z, core), leg: 16 (over y, x).
Axes of the slice: x: 4, y: 4, z: 8, core: 2. Of those that a mesh axis runs over, the one named last changes fastest.
Arguments:
- tensor_low: bfloat16 [16, 256, 256, 256], P('leaf', None, 'leg'), may hold values from -0.0234375 to 0.0234375
- tensor_mid: bfloat16 [16, 256, 128, 256], P('leaf', None, 'leg'), may hold values from -0.0234375 to 0.0234375
- tensor_top: bfloat16 [16, 256, 64, 256], P('leaf', None, 'leg'), may hold values from -0.0234375 to 0.0234375
- child_operators: bfloat16 [16, 2, 4, 256, 256], P('leaf'), may hold values from -6 to 6
- term_choice: int32 [16, 2, 2], P('leaf'), may hold values from 0 to 3
Outputs:
- top_operators: float32 [16, 2, 64, 256], P('leaf', None, 'leg')
The draws below stay inside these ranges and needn't reach their ends.
All inputs are finite; a program needn't handle non-finite values.
Results may differ from the reference program's by a relative error of at most 0.019.
Values may be sent and summed in bfloat16 or wider, within the bound.
A program may use at most 64 MiB of HBM per device.

```python
import jax
import jax.numpy as jnp
from jax import lax

BOND = 256
KOPS = 4
NODES_A = 16
NODES_B = 8
NODES_C = 4
N_LEG = 16


def plant(values, own_key, smallest, high):
    longest = values.shape.index(max(values.shape))
    spots = []
    for shift in (0, 1):
        where = [jax.random.randint(jax.random.fold_in(own_key, axis), (), 0, length) for axis, length in enumerate(values.shape)]
        where[longest] = (where[longest] + shift) % values.shape[longest]
        spots.append(tuple(where))
    return values.at[spots[0]].set(smallest).at[spots[1]].set(high)


def levels(key, shape, split, smallest, high):
    gain, own = 1.0, jax.random.fold_in(key, 6)
    for axis_at, parts in split:
        heights = jnp.exp(jax.random.uniform(jax.random.fold_in(own, axis_at), (parts,), jnp.float32, smallest / len(split), high / len(split)))
        gain = gain * jnp.repeat(heights, shape[axis_at] // parts).reshape([-1 if axis == axis_at else 1 for axis in range(len(shape))])
    return gain


def bell_draw(key, shape, scale, reach, cuts=(), held_as=jnp.bfloat16):
    result = jax.random.normal(key, shape, jnp.float32) * scale
    if len(cuts) > 0:
        result = levels(key, shape, cuts, -0.22, 0.18) * result
    return jnp.clip(result, min=-reach, max=reach).astype(held_as)


def setup_inputs(seed: int = 0) -> dict:
    streams_of = jax.random.split(jax.random.key(seed), 6)
    tensor_low = bell_draw(streams_of[0], (NODES_A, BOND, BOND, BOND), (BOND * BOND) ** -0.5, 0.0234375, ((0, 16), (2, 16)))
    tensor_mid = bell_draw(streams_of[1], (2 * NODES_B, BOND, BOND // 2, BOND), (BOND * BOND) ** -0.5, 0.0234375, ((0, 16), (2, 16)))
    tensor_top = bell_draw(streams_of[2], (4 * NODES_C, BOND, BOND // 4, BOND), (BOND * BOND) ** -0.5, 0.0234375, ((0, 16), (2, 16)))
    child_operators = bell_draw(streams_of[3], (NODES_A, 2, KOPS, BOND, BOND), 1.0, 6.0, ((0, 16),))
    term_choice = plant(jax.random.randint(streams_of[4], (NODES_A, 2, 2), 0, KOPS), jax.random.fold_in(streams_of[4], 1), 0, KOPS - 1).astype(jnp.int32)
    return {"tensor_low": tensor_low, "tensor_mid": tensor_mid, "tensor_top": tensor_top, "child_operators": child_operators, "term_choice": term_choice}


def assemble(blocked):
    parts_count, bond_size, part_width, depth_size = blocked.shape
    slice_width = part_width // N_LEG
    arranged = blocked.reshape(parts_count, bond_size, N_LEG, slice_width, depth_size)
    arranged = jnp.transpose(arranged, (1, 2, 0, 3, 4))
    return arranged.reshape(bond_size, parts_count * part_width, depth_size)


def renormalize(tensor, left_operator, operator_on_right):
    broad_tensor = tensor.astype(jnp.float32)
    blended_terms = jnp.einsum('lm,lra->mra', left_operator.astype(jnp.float32), broad_tensor).astype(jnp.bfloat16)
    rotated_tensor = jnp.einsum('tbe,bw->twe', blended_terms.astype(jnp.float32), operator_on_right.astype(jnp.float32)).astype(jnp.bfloat16)
    return jnp.einsum('orc,orh->ch', rotated_tensor.astype(jnp.float32), broad_tensor)


def renormalize_level(stored, left_ops, right_ops, parts_count):
    node_count = stored.shape[0] // parts_count
    blocked = stored.reshape((node_count, parts_count) + stored.shape[1:])

    def per_node(node_items):
        block_of_nodes, left_node, right_node = node_items
        tensor = assemble(block_of_nodes)
        return jnp.stack([renormalize(tensor, left_node[term_index], right_node[term_index]) for term_index in range(2)])

    return lax.map(per_node, (blocked, left_ops, right_ops))


def select_operators(operator_bank, chosen_operators):
    return jnp.stack([jnp.stack([operator_bank[side_index][chosen_operators[term_index, side_index]] for side_index in range(2)]) for term_index in range(2)])


def reference(tensor_low, tensor_mid, tensor_top, child_operators, term_choice):
    paired = jax.vmap(select_operators)(child_operators, term_choice)
    level_low = renormalize_level(tensor_low, paired[:, :, 0], paired[:, :, 1], 1).astype(jnp.bfloat16)
    level_mid = renormalize_level(tensor_mid, level_low[0::2], level_low[1::2], 2).astype(jnp.bfloat16)
    level_top = renormalize_level(tensor_top, level_mid[0::2], level_mid[1::2], 4)
    node_count = level_top.shape[0]
    bond_size = level_top.shape[-1]
    arranged = level_top.reshape(node_count, 2, 4, bond_size // 4, bond_size)
    arranged = jnp.transpose(arranged, (0, 2, 1, 3, 4))
    return arranged.reshape(node_count * 4, 2, bond_size // 4, bond_size)
```

```python
import jax
import jax.numpy as jnp
from jax import lax
from jax.experimental import pallas as pl
from jax.experimental.pallas import tpu as pltpu
from jax.sharding import PartitionSpec as P

BF, F32 = jnp.bfloat16, jnp.float32
MESH = pl.DeviceIdType.MESH
BOND = 256
LEGS = 16


def x_near(leg):
    x = leg % 4
    return leg // 4 * 4 + x + 1 - 2 * (x % 2)


def x_far(leg):
    return leg // 4 * 4 + 3 - leg % 4


def y_near(leg):
    y = leg // 4
    return (y + 1 - 2 * (y % 2)) * 4 + leg % 4


def y_far(leg):
    return (3 - leg // 4) * 4 + leg % 4


def pick(core, first, second):
    return first + (second - first) * core


def rows_at(start, size):
    return pl.ds(pl.multiple_of(start, 8), size)


class Level:
    def __init__(self, env, ws, wl, sems, own_rows, own_at, left_bits, gather, spread, halves):
        self.env, self.ws, self.wl = env, ws, wl
        self.a_sem, self.b1_sem, self.bd_sem, self.br_sem, self.loc_sem, self.share_sem = sems
        self.own_rows, self.own_at = own_rows, own_at
        self.n_left = own_rows // 4
        self.left_at = own_at + left_bits * self.n_left
        self.halves, self.part = halves, 16 // halves
        core, leg = env["core"], env["leg"]
        fx, fy = gather
        gx, gy = spread
        self.slot_legs = [leg, fx(leg), fy(leg), fx(fy(leg))]
        self.a1 = pick(core, fx(leg), fy(leg))
        self.a2 = pick(core, fy(leg), fx(leg))
        self.first, self.second = 1 + core, 2 - core
        self.b1 = lambda one: pick(core, gy(one), gx(one))
        self.b2 = lambda one: pick(core, gx(one), gy(one))
        self.leg_of = {"own": leg, "first": self.a1, "second": self.a2, "both": fx(fy(leg))}
        self.slot_of = {"own": 0, "first": self.first, "second": self.second, "both": 3}
        self.pending = []

    def remote(self, src, dst, sem, index, to):
        return pltpu.make_async_remote_copy(
            src_ref=src,
            dst_ref=dst,
            send_sem=sem.at[(0, *index)],
            recv_sem=sem.at[(1, *index)],
            device_id=to,
            device_id_type=MESH,
        )

    def go(self, copy):
        copy.start()
        self.pending.append(copy)

    def block(self, slot, h):
        return self.ws.at[
            slot, rows_at(self.own_at, self.own_rows), pl.ds(h * self.part, self.part), :
        ]

    def piece(self, slot, h):
        return self.ws.at[
            slot, rows_at(self.left_at, self.n_left), pl.ds(h * self.part, self.part), :
        ]

    def place(self, one, h):
        return self.wl.at[:, rows_at(one * 16 + h * self.part, self.part), :]

    def to(self, one):
        return (self.env["leaf"], one)

    def hop(self, kind, h, arriving):
        src = {"a1": 0, "own": 0, "relay": self.first}[kind]
        dst = {"a1": self.first, "own": self.second, "relay": 3}[kind]
        target = self.a1 if kind == "a1" else self.a2
        index = ({"a1": 0, "own": 1, "relay": 2}[kind], h)
        source = self.block(dst if arriving else src, h)
        return self.remote(source, self.block(dst, h), self.a_sem, index, self.to(target))

    def send_hop(self, kind, h):
        self.go(self.hop(kind, h, False))

    def recv_hop(self, kind, h):
        self.hop(kind, h, True).wait_recv()

    def spread(self, name, h):
        slot, one = self.slot_of[name], self.leg_of[name]
        piece, place, leg = self.piece(slot, h), self.place(one, h), self.env["leg"]
        self.go(self.remote(piece, place, self.b1_sem, (slot, h), self.to(self.b1(leg))))
        self.go(self.remote(piece, place, self.bd_sem, (slot, h), self.to(self.b2(leg))))
        copy = pltpu.make_async_copy(piece, place, self.loc_sem.at[slot, h])
        copy.start()
        self.pending.append(copy)

    def relay(self, name, h):
        slot, leg = self.slot_of[name], self.env["leg"]
        place = self.place(self.b1(self.leg_of[name]), h)
        self.remote(place, place, self.b1_sem, (slot, h), self.to(self.b1(leg))).wait_recv()
        self.go(self.remote(place, place, self.br_sem, (slot, h), self.to(self.b2(leg))))

    def arrive(self, name, h):
        slot, leg, one = self.slot_of[name], self.env["leg"], self.leg_of[name]
        place = self.place(self.b2(one), h)
        self.remote(place, place, self.bd_sem, (slot, h), self.to(self.b2(leg))).wait_recv()
        place = self.place(self.b2(self.b1(one)), h)
        self.remote(place, place, self.br_sem, (slot, h), self.to(self.b2(leg))).wait_recv()

    def finish(self):
        for copy in self.pending:
            if copy.is_remote:
                copy.wait_send()

    def finish_local(self):
        for copy in self.pending:
            if not copy.is_remote:
                copy.wait()

    def share(self, name, step, start, size, to):
        slot = self.slot_of[name]
        span = self.ws.at[slot, rows_at(start, size)]
        self.go(self.remote(span, span, self.share_sem, (step, slot), to))

    def shared(self, name, step, start, size, to):
        slot = self.slot_of[name]
        span = self.ws.at[slot, rows_at(start, size)]
        self.remote(span, span, self.share_sem, (step, slot), to).wait_recv()


def transfer(src, dst, sem, index, to):
    return pltpu.make_async_remote_copy(
        src_ref=src,
        dst_ref=dst,
        send_sem=sem.at[(0, *index)],
        recv_sem=sem.at[(1, *index)],
        device_id=to,
        device_id_type=MESH,
    )


def kernel(
    w_low, w_mid, w_top, left_in, right_in, out,
    ws_low, ws_mid, ws_top, wl_low, wl_mid, wl_top, top_parts, flat_0, flat_1, ys_0, ys_1, zs, acc, l_cat, r_cat,
    right_t, sums, inbox, block, ops_a, mate_in, mid_sum, mid_in, mid_block, ops_b,
    low_a, low_b1, low_bd, low_br, low_loc, low_share,
    mid_a, mid_b1, mid_bd, mid_br, mid_loc, mid_share,
    top_a, top_b1, top_bd, top_br, top_loc, top_share,
    first_sem, mid_first, top_first, rs_sem, ag_sem, op_sem,
    mate_sem, rs2_sem, ag2_sem, op2_sem, half_sem, quarter_sem, rs3_sem,
    half_in, half_sum, quarter_in, rows_out, rows_in,
):
    leaf, leg = lax.axis_index("leaf"), lax.axis_index("leg")
    core, z = leaf % 2, leaf // 2
    side = z % 2
    x, y = leg % 4, leg // 4
    far_x, far_y = x // 2, y // 2
    near_x, near_y = (x + far_x) % 2, (y + far_y) % 2
    mate = (leaf + 1 - 2 * core, leg)
    across = (leaf + 2 - 4 * side, leg)
    cross = (leaf + 2 - 4 * side + 1 - 2 * core, leg)
    env = {"leaf": leaf, "leg": leg, "core": core}

    barrier = pltpu.get_barrier_semaphore()

    @pl.loop(1, LEGS)
    def _(d):
        pl.semaphore_signal(barrier, inc=1, device_id=(leaf, (leg + d) % LEGS), device_id_type=MESH)

    for peer in (mate, across, cross):
        pl.semaphore_signal(barrier, inc=1, device_id=peer, device_id_type=MESH)
    pl.semaphore_wait(barrier, LEGS + 2)

    low = Level(
        env, ws_low, wl_low, (low_a, low_b1, low_bd, low_br, low_loc, low_share),
        256, 0, near_x + 2 * near_y, (x_near, y_near), (x_far, y_far), 2,
    )
    mid = Level(
        env, ws_mid, wl_mid, (mid_a, mid_b1, mid_bd, mid_br, mid_loc, mid_share),
        128, core * 128, far_x + 2 * far_y, (x_far, y_far), (x_near, y_near), 1,
    )
    top = Level(
        env, ws_top, wl_top, (top_a, top_b1, top_bd, top_br, top_loc, top_share),
        64, core * 128 + side * 64, near_x + 2 * near_y, (x_near, y_near), (x_far, y_far), 1,
    )

    own_low = pltpu.make_async_copy(w_low, ws_low.at[0], first_sem.at[0])
    own_low.start()
    mine = pl.ds(pl.multiple_of(core * 8, 8), 8)
    theirs = pl.ds(pl.multiple_of(8 - core * 8, 8), 8)
    mid_rows, mate_rows = rows_at(core * 128, 128), rows_at(128 - core * 128, 128)
    mid_out = transfer(
        w_mid.at[mate_rows], ws_mid.at[0, mate_rows, mine, :], mid_first, (0,), mate
    )
    mid_out.start()
    own_mid = pltpu.make_async_copy(
        w_mid.at[mid_rows], ws_mid.at[0, mid_rows, mine, :], first_sem.at[1]
    )
    own_mid.start()
    q = side * 2 + core
    quarters = [
        ((1 - core) * 128 + side * 64, side * 2 + 1 - core, mate),
        (core * 128 + (1 - side) * 64, (1 - side) * 2 + core, across),
        ((1 - core) * 128 + (1 - side) * 64, (1 - side) * 2 + 1 - core, cross),
    ]
    top_sends = []
    for n, (start, _, peer) in enumerate(quarters):
        copy = transfer(w_top.at[rows_at(start, 64)], top_parts.at[q], top_first, (n,), peer)
        copy.start()
        top_sends.append(copy)
    own_top = pltpu.make_async_copy(
        w_top.at[rows_at(top.own_at, 64)], top_parts.at[q], first_sem.at[2]
    )
    own_top.start()

    def load_left(ref, n_left, at):
        for t in range(2):
            l_cat[t * n_left : (t + 1) * n_left] = ref[t, rows_at(at, n_left), :]

    def load_right(ref, legs):
        for t in range(2):
            for slot, one in enumerate(legs):
                start = t * 64 + slot * 16
                r_cat[start : start + 16] = ref[t, rows_at(one * 16, 16), :]

    def mix_left(level, name):
        slot, n_left = level.slot_of[name], level.n_left

        @pl.loop(0, 16)
        def _(n):
            rows = level.ws[slot, pl.ds(n * 16, 16), :, :]
            rows = rows.reshape(256, BOND).astype(F32)
            for n_col, ref in enumerate((flat_0, flat_1)):
                ref[pl.ds(n * 256, 256), :] = rows[:, n_col * 128 : n_col * 128 + 128]

        left = l_cat[: 2 * n_left]

        @pl.loop(0, 16)
        def _(s):
            for source, target in ((flat_0, ys_0), (flat_1, ys_1)):
                rows = source[pl.ds(s, 256, stride=16), :].astype(BF)
                target[pl.ds(slot * 16 + s, 2 * n_left, stride=64), :] = jnp.dot(
                    left, rows, preferred_element_type=F32
                )

    def contract(level):
        acc[...] = jnp.zeros_like(acc)
        n_left = level.n_left

        @pl.loop(0, n_left // 4)
        def _(n):
            for k in range(4):
                turned = jnp.dot(
                    r_cat[...], level.wl[n * 4 + k], preferred_element_type=F32
                ).astype(BF)
                for t in range(2):
                    zs[t, k * 64 : (k + 1) * 64] = turned[t * 64 : (t + 1) * 64]
            for t in range(2):
                span = rows_at((t * n_left + n * 4) * 64, 256)
                rows = jnp.concatenate([ys_0[span, :], ys_1[span, :]], axis=1).astype(BF)
                acc[t] += lax.dot_general(
                    zs[t], rows, (((0,), (0,)), ((), ())), preferred_element_type=F32
                )

    def ring_start(src_of, dst_of, sem):
        @pl.loop(1, LEGS)
        def _(d):
            one = (leg + d) % LEGS
            transfer(src_of(one), dst_of(d), sem, (d,), (leaf, one)).start()

    def ring_recv(dst_of, sem):
        @pl.loop(1, LEGS)
        def _(d):
            ref = dst_of(d)
            transfer(ref, ref, sem, (d,), (leaf, (leg + d) % LEGS)).wait_recv()

    def ring_sent(src_of, sem):
        @pl.loop(1, LEGS)
        def _(d):
            one = (leg + d) % LEGS
            ref = src_of(one)
            transfer(ref, ref, sem, (d,), (leaf, one)).wait_send()

    load_left(left_in, low.n_left, low.left_at)
    load_right(right_in, low.slot_legs)
    own_low.wait()
    for h in range(2):
        low.send_hop("a1", h)
    for h in range(2):
        low.spread("own", h)
    own_mid.wait()
    transfer(
        w_mid.at[mid_rows], ws_mid.at[0, mid_rows, theirs, :], mid_first, (0,), mate
    ).wait_recv()
    mid.send_hop("a1", 0)
    mix_left(low, "own")

    own_top.wait()
    for n, (_, part, peer) in enumerate(quarters):
        transfer(
            w_top.at[rows_at(top.own_at, 64)], top_parts.at[part], top_first, (n,), peer
        ).wait_recv()

    @pl.loop(0, 4)
    def _(n):
        for part in range(4):
            half_in[pl.ds(0, 16), part * 4 : part * 4 + 4, :] = top_parts[
                part, pl.ds(n * 16, 16), :, :
            ].astype(F32)
        ws_top[0, rows_at(top.own_at + n * 16, 16), :, :] = half_in[pl.ds(0, 16)].astype(BF)

    for h in range(2):
        low.recv_hop("a1", h)
        low.send_hop("relay", h)
        low.send_hop("own", h)
        low.spread("first", h)
    mid.recv_hop("a1", 0)
    mid.send_hop("relay", 0)
    mid.send_hop("own", 0)
    for name in ("own", "first"):
        mid.spread(name, 0)
        mid.share(name, 0, mid.own_at, 128, mate)
    for h in range(2):
        low.relay("own", h)
    mix_left(low, "first")
    for h in range(2):
        low.relay("first", h)
    for h in range(2):
        low.recv_hop("relay", h)
        low.spread("both", h)
        low.recv_hop("own", h)
        low.spread("second", h)
    top.send_hop("a1", 0)
    mid.relay("own", 0)
    mid.relay("first", 0)
    mix_left(low, "both")
    for h in range(2):
        low.relay("both", h)
    mix_left(low, "second")
    for h in range(2):
        low.relay("second", h)
    mid.recv_hop("relay", 0)
    mid.spread("both", 0)
    mid.share("both", 0, mid.own_at, 128, mate)
    mid.recv_hop("own", 0)
    mid.spread("second", 0)
    mid.share("second", 0, mid.own_at, 128, mate)
    top.recv_hop("a1", 0)
    top.send_hop("relay", 0)
    top.send_hop("own", 0)
    for name in ("own", "first"):
        top.spread(name, 0)
        top.share(name, 0, top.own_at, 64, across)
    for name in ("own", "first", "both", "second"):
        for h in range(2):
            low.arrive(name, h)
    low.finish_local()
    contract(low)

    sums[...] = acc[...].astype(BF)
    ring_start(lambda one: sums.at[:, rows_at(one * 16, 16), :], lambda d: inbox.at[d], rs_sem)
    mid.relay("both", 0)
    mid.relay("second", 0)
    ring_recv(lambda d: inbox.at[d], rs_sem)
    total = acc[:, rows_at(leg * 16, 16), :]
    for d in range(1, LEGS):
        total = total + inbox[d].astype(F32)
    block[...] = total.astype(BF)
    ops_a[core, :, rows_at(leg * 16, 16), :] = total.astype(BF)
    ring_start(
        lambda one: block, lambda d: ops_a.at[core, :, rows_at(leg * 16, 16), :], ag_sem
    )
    top.recv_hop("relay", 0)
    top.spread("both", 0)
    top.share("both", 0, top.own_at, 64, across)
    ring_recv(
        lambda d: ops_a.at[core, :, rows_at((leg - d + LEGS) % LEGS * 16, 16), :], ag_sem
    )
    op_send = transfer(ops_a.at[core], ops_a.at[core], op_sem, (0,), mate)
    op_send.start()
    top.recv_hop("own", 0)
    top.spread("second", 0)
    top.share("second", 0, top.own_at, 64, across)
    top.relay("own", 0)
    top.relay("first", 0)
    transfer(ops_a.at[1 - core], ops_a.at[1 - core], op_sem, (0,), mate).wait_recv()

    load_left(ops_a.at[0], mid.n_left, mid.left_at)
    for t in range(2):
        right_t[t] = ops_a[1, t].T
    load_right(right_t, mid.slot_legs)
    for name in ("own", "first", "both", "second"):
        mid.shared(name, 0, 128 - core * 128, 128, mate)
        mix_left(mid, name)
        top.shared(name, 0, core * 128 + (1 - side) * 64, 64, across)
        top.share(name, 1, core * 128, 128, mate)
        if name in ("both", "second"):
            top.relay(name, 0)
    for name in ("own", "first", "both", "second"):
        mid.arrive(name, 0)
    mid.finish_local()
    contract(mid)

    ring_sent(lambda one: sums.at[:, rows_at(one * 16, 16), :], rs_sem)
    sums[...] = acc[...].astype(BF)
    mate_send = transfer(sums.at[1 - core], mate_in, mate_sem, (0,), mate)
    mate_send.start()
    transfer(mate_in, mate_in, mate_sem, (0,), mate).wait_recv()
    mid_sum[...] = (acc[core] + mate_in[...].astype(F32)).astype(BF)
    ring_start(lambda one: mid_sum.at[rows_at(one * 16, 16), :], lambda d: mid_in.at[d], rs2_sem)
    own_rows = rows_at(leg * 16, 16)
    total = acc[core, own_rows, :] + mate_in[own_rows, :].astype(F32)
    ring_recv(lambda d: mid_in.at[d], rs2_sem)
    for d in range(1, LEGS):
        total = total + mid_in[d].astype(F32)
    mid_block[...] = total.astype(BF)
    ops_b[side, core, own_rows, :] = total.astype(BF)
    ring_start(lambda one: mid_block, lambda d: ops_b.at[side, core, own_rows, :], ag2_sem)
    ring_recv(
        lambda d: ops_b.at[side, core, rows_at((leg - d + LEGS) % LEGS * 16, 16), :], ag2_sem
    )
    ours = ops_b.at[side, core]
    op2_sends = [
        transfer(ours, ours, op2_sem, (0,), mate),
        transfer(ours, ours, op2_sem, (1,), across),
    ]
    for copy in op2_sends:
        copy.start()
    other = ops_b.at[1 - side, core]
    transfer(other, other, op2_sem, (1,), across).wait_recv()
    op2_sends.append(transfer(other, other, op2_sem, (2,), mate))
    op2_sends[-1].start()
    for n, ref in ((0, ops_b.at[side, 1 - core]), (2, ops_b.at[1 - side, 1 - core])):
        transfer(ref, ref, op2_sem, (n,), mate).wait_recv()

    load_left(ops_b.at[0], top.n_left, top.left_at)
    for t in range(2):
        right_t[t] = ops_b[1, t].T
    load_right(right_t, top.slot_legs)
    for name in ("own", "first", "both", "second"):
        top.shared(name, 1, 128 - core * 128, 128, mate)
        mix_left(top, name)
    for name in ("own", "first", "both", "second"):
        top.arrive(name, 0)
    top.finish_local()
    contract(top)

    half_sends = []
    for n in range(2):
        copy = transfer(
            acc.at[:, rows_at((2 * n + 1 - core) * 64, 64), :],
            quarter_in.at[n],
            half_sem, (n,), mate,
        )
        copy.start()
        half_sends.append(copy)
    for n in range(2):
        transfer(quarter_in.at[n], quarter_in.at[n], half_sem, (n,), mate).wait_recv()
        half_sum[n] = acc[:, rows_at((2 * n + core) * 64, 64), :] + quarter_in[n]
    side_send = transfer(half_sum.at[1 - side], quarter_in.at[2], quarter_sem, (0,), across)
    side_send.start()
    transfer(quarter_in.at[2], quarter_in.at[2], quarter_sem, (0,), across).wait_recv()
    for t in range(2):
        part = half_sum[side, t] + quarter_in[2, t]
        for one in range(LEGS):
            rows_out[one, t * 4 : t * 4 + 4, :] = part[one * 4 : one * 4 + 4]
    ring_start(lambda one: rows_out.at[one], lambda d: rows_in.at[d], rs3_sem)
    total = rows_out[leg]
    ring_recv(lambda d: rows_in.at[d], rs3_sem)
    for d in range(1, LEGS):
        total = total + rows_in[d]
    for t in range(2):
        out[0, t] = total[t * 4 : t * 4 + 4]

    for level in (low, mid, top):
        level.finish()
    mid_out.wait_send()
    for copy in (*top_sends, op_send, mate_send, *op2_sends, *half_sends, side_send):
        copy.wait_send()
    ring_sent(lambda one: block, ag_sem)
    ring_sent(lambda one: mid_sum.at[rows_at(one * 16, 16), :], rs2_sem)
    ring_sent(lambda one: mid_block, ag2_sem)
    ring_sent(lambda one: rows_out.at[one], rs3_sem)


def on_device(tensor_low, tensor_mid, tensor_top, child_operators, term_choice):
    bank, choice = child_operators[0], term_choice[0]

    def chosen(side):
        return jnp.stack(
            [
                lax.dynamic_index_in_dim(bank[side], choice[t, side], 0, keepdims=False)
                for t in range(2)
            ]
        )

    left, right = chosen(0), jnp.swapaxes(chosen(1), 1, 2)
    dma, vmem = pltpu.SemaphoreType.DMA, pltpu.VMEM

    def level_sems(halves):
        return [
            dma((2, 3, halves)),
            dma((2, 4, halves)),
            dma((2, 4, halves)),
            dma((2, 4, halves)),
            dma((4, halves)),
            dma((2, 2, 4)),
        ]

    hbm = pl.BlockSpec(memory_space=pl.ANY)
    inside = pl.BlockSpec(memory_space=pltpu.VMEM)
    return pl.pallas_call(
        kernel,
        out_shape=jax.ShapeDtypeStruct((1, 2, 4, BOND), F32),
        in_specs=[hbm, hbm, hbm, inside, inside],
        out_specs=inside,
        scratch_shapes=[
            vmem((4, 256, 16, BOND), BF),
            vmem((4, 256, 16, BOND), BF),
            vmem((4, 256, 16, BOND), BF),
            vmem((64, 256, BOND), BF),
            vmem((32, 256, BOND), BF),
            vmem((16, 256, BOND), BF),
            vmem((4, 64, 4, BOND), BF),
            vmem((4096, 128), F32),
            vmem((4096, 128), F32),
            vmem((8192, 128), F32),
            vmem((8192, 128), F32),
            vmem((2, 256, BOND), BF),
            vmem((2, BOND, BOND), F32),
            vmem((128, BOND), BF),
            vmem((128, BOND), BF),
            vmem((2, BOND, BOND), BF),
            vmem((2, BOND, BOND), BF),
            vmem((LEGS, 2, 16, BOND), BF),
            vmem((2, 16, BOND), BF),
            vmem((2, 2, BOND, BOND), BF),
            vmem((BOND, BOND), BF),
            vmem((BOND, BOND), BF),
            vmem((LEGS, 16, BOND), BF),
            vmem((16, BOND), BF),
            vmem((2, 2, BOND, BOND), BF),
            *level_sems(2),
            *level_sems(1),
            *level_sems(1),
            dma((3,)),
            dma((2, 1)),
            dma((2, 3)),
            dma((2, LEGS)),
            dma((2, LEGS)),
            dma((2, 1)),
            dma((2, 1)),
            dma((2, LEGS)),
            dma((2, LEGS)),
            dma((2, 3)),
            dma((2, 2)),
            dma((2, 1)),
            dma((2, LEGS)),
            vmem((16, 16, BOND), F32),
            vmem((2, 2, 64, BOND), F32),
            vmem((3, 2, 64, BOND), F32),
            vmem((LEGS, 8, BOND), F32),
            vmem((LEGS, 8, BOND), F32),
        ],
        compiler_params=pltpu.CompilerParams(
            collective_id=0, has_side_effects=True, vmem_limit_bytes=67043328
        ),
    )(tensor_low[0], tensor_mid[0], tensor_top[0], left, right)


def solution(mesh):
    return jax.shard_map(
        on_device,
        mesh=mesh,
        in_specs=(
            P("leaf", None, "leg", None),
            P("leaf", None, "leg", None),
            P("leaf", None, "leg", None),
            P("leaf", None, None, None, None),
            P("leaf", None, None),
        ),
        out_specs=P("leaf", None, "leg", None),
        check_vma=False,
    )
```

```python
import jax
import jax.numpy as jnp
from jax import lax
from jax.experimental import pallas as pl
from jax.experimental.pallas import tpu as pltpu
from jax.sharding import PartitionSpec as P

BF, F32 = jnp.bfloat16, jnp.float32
MESH = pl.DeviceIdType.MESH
BOND = 256
LEGS = 16


def x_near(leg):
    x = leg % 4
    return leg // 4 * 4 + x + 1 - 2 * (x % 2)


def x_far(leg):
    return leg // 4 * 4 + 3 - leg % 4


def y_near(leg):
    y = leg // 4
    return (y + 1 - 2 * (y % 2)) * 4 + leg % 4


def y_far(leg):
    return (3 - leg // 4) * 4 + leg % 4


def pick(core, first, second):
    return first + (second - first) * core


def rows_at(start, size):
    return pl.ds(pl.multiple_of(start, 8), size)


class Level:
    def __init__(self, env, ws, wl, sems, own_rows, own_at, left_bits, gather, spread, halves):
        self.env, self.ws, self.wl = env, ws, wl
        self.a_sem, self.b1_sem, self.bd_sem, self.br_sem, self.loc_sem, self.share_sem = sems
        self.own_rows, self.own_at = own_rows, own_at
        self.n_left = own_rows // 4
        self.left_at = own_at + left_bits * self.n_left
        self.halves, self.part = halves, 16 // halves
        core, leg = env["core"], env["leg"]
        fx, fy = gather
        gx, gy = spread
        self.slot_legs = [leg, fx(leg), fy(leg), fx(fy(leg))]
        self.a1 = pick(core, fx(leg), fy(leg))
        self.a2 = pick(core, fy(leg), fx(leg))
        self.first, self.second = 1 + core, 2 - core
        self.b1 = lambda one: pick(core, gy(one), gx(one))
        self.b2 = lambda one: pick(core, gx(one), gy(one))
        self.leg_of = {"own": leg, "first": self.a1, "second": self.a2, "both": fx(fy(leg))}
        self.slot_of = {"own": 0, "first": self.first, "second": self.second, "both": 3}
        self.pending = []

    def remote(self, src, dst, sem, index, to):
        return pltpu.make_async_remote_copy(
            src_ref=src,
            dst_ref=dst,
            send_sem=sem.at[(0, *index)],
            recv_sem=sem.at[(1, *index)],
            device_id=to,
            device_id_type=MESH,
        )

    def go(self, copy):
        copy.start()
        self.pending.append(copy)

    def block(self, slot, h):
        return self.ws.at[
            slot, rows_at(self.own_at, self.own_rows), pl.ds(h * self.part, self.part), :
        ]

    def piece(self, slot, h):
        return self.ws.at[
            slot, rows_at(self.left_at, self.n_left), pl.ds(h * self.part, self.part), :
        ]

    def place(self, one, h):
        return self.wl.at[:, rows_at(one * 16 + h * self.part, self.part), :]

    def to(self, one):
        return (self.env["leaf"], one)

    def hop(self, kind, h, arriving):
        src = {"a1": 0, "own": 0, "relay": self.first}[kind]
        dst = {"a1": self.first, "own": self.second, "relay": 3}[kind]
        target = self.a1 if kind == "a1" else self.a2
        index = ({"a1": 0, "own": 1, "relay": 2}[kind], h)
        source = self.block(dst if arriving else src, h)
        return self.remote(source, self.block(dst, h), self.a_sem, index, self.to(target))

    def send_hop(self, kind, h):
        self.go(self.hop(kind, h, False))

    def recv_hop(self, kind, h):
        self.hop(kind, h, True).wait_recv()

    def spread(self, name, h):
        slot, one = self.slot_of[name], self.leg_of[name]
        piece, place, leg = self.piece(slot, h), self.place(one, h), self.env["leg"]
        self.go(self.remote(piece, place, self.b1_sem, (slot, h), self.to(self.b1(leg))))
        self.go(self.remote(piece, place, self.bd_sem, (slot, h), self.to(self.b2(leg))))
        copy = pltpu.make_async_copy(piece, place, self.loc_sem.at[slot, h])
        copy.start()
        self.pending.append(copy)

    def relay(self, name, h):
        slot, leg = self.slot_of[name], self.env["leg"]
        place = self.place(self.b1(self.leg_of[name]), h)
        self.remote(place, place, self.b1_sem, (slot, h), self.to(self.b1(leg))).wait_recv()
        self.go(self.remote(place, place, self.br_sem, (slot, h), self.to(self.b2(leg))))

    def arrive(self, name, h):
        slot, leg, one = self.slot_of[name], self.env["leg"], self.leg_of[name]
        place = self.place(self.b2(one), h)
        self.remote(place, place, self.bd_sem, (slot, h), self.to(self.b2(leg))).wait_recv()
        place = self.place(self.b2(self.b1(one)), h)
        self.remote(place, place, self.br_sem, (slot, h), self.to(self.b2(leg))).wait_recv()

    def finish(self):
        for copy in self.pending:
            if copy.is_remote:
                copy.wait_send()

    def finish_local(self):
        for copy in self.pending:
            if not copy.is_remote:
                copy.wait()

    def share(self, name, step, start, size, to):
        slot = self.slot_of[name]
        span = self.ws.at[slot, rows_at(start, size)]
        self.go(self.remote(span, span, self.share_sem, (step, slot), to))

    def shared(self, name, step, start, size, to):
        slot = self.slot_of[name]
        span = self.ws.at[slot, rows_at(start, size)]
        self.remote(span, span, self.share_sem, (step, slot), to).wait_recv()


def transfer(src, dst, sem, index, to):
    return pltpu.make_async_remote_copy(
        src_ref=src,
        dst_ref=dst,
        send_sem=sem.at[(0, *index)],
        recv_sem=sem.at[(1, *index)],
        device_id=to,
        device_id_type=MESH,
    )


def kernel(
    w_low, w_mid, w_top, bank_in, choice, out,
    ws_low, ws_mid, ws_top, wl_low, wl_mid, wl_top, top_parts, by_row_low, by_row_mid, ys_0, ys_1,
    zs, acc, l_cat, r_cat, right_t, bank, sums, inbox, block, ops_a, mate_in, mid_sum, mid_in,
    mid_block, ops_b,
    low_a, low_b1, low_bd, low_br, low_loc, low_share,
    mid_a, mid_b1, mid_bd, mid_br, mid_loc, mid_share,
    top_a, top_b1, top_bd, top_br, top_loc, top_share,
    first_sem, mid_first, top_first, rs_sem, ag_sem, op_sem,
    mate_sem, rs2_sem, ag2_sem, op2_sem, half_sem, quarter_sem, rs3_sem,
    wide, half_sum, half_in, side_sum, side_in, rows_out, rows_in,
):
    leaf, leg = lax.axis_index("leaf"), lax.axis_index("leg")
    core, z = leaf % 2, leaf // 2
    side = z % 2
    x, y = leg % 4, leg // 4
    far_x, far_y = x // 2, y // 2
    near_x, near_y = (x + far_x) % 2, (y + far_y) % 2
    mate = (leaf + 1 - 2 * core, leg)
    across = (leaf + 2 - 4 * side, leg)
    cross = (leaf + 2 - 4 * side + 1 - 2 * core, leg)
    env = {"leaf": leaf, "leg": leg, "core": core}
    near, far = (x_near, y_near), (x_far, y_far)

    low = Level(
        env, ws_low, wl_low, (low_a, low_b1, low_bd, low_br, low_loc, low_share),
        256, 0, near_x + 2 * near_y, near, far, 2,
    )
    mid = Level(
        env, ws_mid, wl_mid, (mid_a, mid_b1, mid_bd, mid_br, mid_loc, mid_share),
        128, core * 128, near_x + 2 * near_y, near, far, 1,
    )
    top = Level(
        env, ws_top, wl_top, (top_a, top_b1, top_bd, top_br, top_loc, top_share),
        64, core * 128 + side * 64, far_x + 2 * far_y, far, near, 1,
    )
    q = side * 2 + core
    mine, theirs = rows_at(core * 8, 8), rows_at(8 - core * 8, 8)
    mid_rows, mate_rows = rows_at(core * 128, 128), rows_at(128 - core * 128, 128)

    own_low = [
        pltpu.make_async_copy(
            w_low.at[:, pl.ds(h * 8, 8), :], ws_low.at[0, :, pl.ds(h * 8, 8), :], first_sem.at[h]
        )
        for h in range(2)
    ]
    own_mid = pltpu.make_async_copy(
        w_mid.at[mid_rows], ws_mid.at[0, mid_rows, mine, :], first_sem.at[2]
    )
    own_top = pltpu.make_async_copy(
        w_top.at[rows_at(top.own_at, 64)], top_parts.at[q], first_sem.at[3]
    )
    own_bank = pltpu.make_async_copy(bank_in, bank, first_sem.at[4])
    for copy in (*own_low, own_bank, own_mid, own_top):
        copy.start()

    barrier = pltpu.get_barrier_semaphore()

    @pl.loop(1, LEGS)
    def _(d):
        pl.semaphore_signal(barrier, inc=1, device_id=(leaf, (leg + d) % LEGS), device_id_type=MESH)

    for peer in (mate, across, cross):
        pl.semaphore_signal(barrier, inc=1, device_id=peer, device_id_type=MESH)
    pl.semaphore_wait(barrier, LEGS + 2)

    for h in range(2):
        own_low[h].wait()
        low.send_hop("a1", h)
    mid_out = transfer(
        w_mid.at[mate_rows], ws_mid.at[0, mate_rows, mine, :], mid_first, (0,), mate
    )
    mid_out.start()
    quarters = [
        ((1 - core) * 128 + side * 64, side * 2 + 1 - core, mate),
        (core * 128 + (1 - side) * 64, (1 - side) * 2 + core, across),
        ((1 - core) * 128 + (1 - side) * 64, (1 - side) * 2 + 1 - core, cross),
    ]
    top_sends = []
    for n, (start, _, peer) in enumerate(quarters):
        copy = transfer(w_top.at[rows_at(start, 64)], top_parts.at[q], top_first, (n,), peer)
        copy.start()
        top_sends.append(copy)
    for h in range(2):
        low.spread("own", h)

    def load_left(read, n_left, at):
        for t in range(2):
            l_cat[t * n_left : (t + 1) * n_left] = read(t, rows_at(at, n_left))

    def load_right(legs):
        for t in range(2):
            for slot, one in enumerate(legs):
                start = t * 64 + slot * 16
                r_cat[start : start + 16] = right_t[t, rows_at(one * 16, 16), :]

    def mix_rows(slot, s, rows, n_left):
        mixed = jnp.dot(l_cat[: 2 * n_left], rows, preferred_element_type=F32)
        span = pl.ds(slot * 16 + s, 2 * n_left, stride=64)
        ys_0[span, :] = mixed[:, :128]
        ys_1[span, :] = mixed[:, 128:]

    def mix_low(name):
        slot = low.slot_of[name]

        @pl.loop(0, 16, unroll=2)
        def _(n):
            by_row_low[:, pl.ds(n * 16, 16), :] = jnp.swapaxes(ws_low[slot, pl.ds(n * 16, 16)], 0, 1)

        @pl.loop(0, 16, unroll=4)
        def _(s):
            mix_rows(slot, s, by_row_low[s], low.n_left)

    def turn_mid(name, half):
        slot = mid.slot_of[name]

        @pl.loop(0, 8, unroll=2)
        def _(n):
            rows = rows_at(half * 128 + n * 16, 16)
            by_row_mid[pl.ds(slot * 16, 16), rows, :] = jnp.swapaxes(ws_mid[slot, rows], 0, 1)

    def mix_mid():
        @pl.loop(0, 64, unroll=8)
        def _(s):
            mix_rows(0, s, by_row_mid[s], mid.n_left)

    def turn_top(name):
        slot = top.slot_of[name]

        @pl.loop(0, 16, unroll=2)
        def _(n):
            turned = jnp.swapaxes(ws_top[slot, pl.ds(n * 16, 16)], 0, 1)
            for s in range(16):
                ws_low[slot, s * 16 + n] = turned[s]

    def mix_top():
        @pl.loop(0, 64, unroll=8)
        def _(s):
            rows = ws_low[s // 16, pl.ds(s % 16 * 16, 16)]
            mix_rows(0, s, rows.reshape(256, BOND), top.n_left)

    def contract(level):
        acc[...] = jnp.zeros_like(acc)
        n_left = level.n_left

        @pl.loop(0, n_left // 4, unroll=2)
        def _(n):
            for k in range(4):
                turned = jnp.dot(
                    r_cat[...], level.wl[n * 4 + k], preferred_element_type=F32
                ).astype(BF)
                for t in range(2):
                    zs[n % 2, t, k * 64 : (k + 1) * 64] = turned[t * 64 : (t + 1) * 64]
            for t in range(2):
                span = rows_at((t * n_left + n * 4) * 64, 256)
                rows = jnp.concatenate([ys_0[span, :], ys_1[span, :]], axis=1).astype(BF)
                acc[t] += lax.dot_general(
                    zs[n % 2, t], rows, (((0,), (0,)), ((), ())), preferred_element_type=F32
                )

    def ring_start(src_of, dst_of, sem):
        @pl.loop(1, LEGS)
        def _(d):
            one = (leg + d) % LEGS
            transfer(src_of(one), dst_of(d), sem, (d,), (leaf, one)).start()

    def ring_recv(dst_of, sem):
        @pl.loop(1, LEGS)
        def _(d):
            ref = dst_of(d)
            transfer(ref, ref, sem, (d,), (leaf, (leg + d) % LEGS)).wait_recv()

    def ring_sent(src_of, sem):
        @pl.loop(1, LEGS)
        def _(d):
            one = (leg + d) % LEGS
            ref = src_of(one)
            transfer(ref, ref, sem, (d,), (leaf, one)).wait_send()

    def mid_share(name):
        mid.share(name, 0, mid.own_at, 128, mate)

    def mid_shared(name):
        mid.shared(name, 0, 128 - core * 128, 128, mate)

    def top_across(name):
        top.shared(name, 0, core * 128 + (1 - side) * 64, 64, across)
        top.share(name, 1, core * 128, 128, mate)

    own_top.wait()
    for n, (_, part, peer) in enumerate(quarters):
        transfer(
            w_top.at[rows_at(top.own_at, 64)], top_parts.at[part], top_first, (n,), peer
        ).wait_recv()

    @pl.loop(0, 4)
    def _(n):
        for part in range(4):
            wide[:, part * 4 : part * 4 + 4, :] = top_parts[part, pl.ds(n * 16, 16), :, :].astype(
                F32
            )
        ws_top[0, rows_at(top.own_at + n * 16, 16), :, :] = wide[:, :16, :].astype(BF)

    own_bank.wait()
    load_left(lambda t, rows: bank[0, choice[t, 0], rows, :], low.n_left, low.left_at)
    for t in range(2):
        right_t[t] = bank[1, choice[t, 1]].T
    load_right(low.slot_legs)
    top.send_hop("a1", 0)
    own_mid.wait()
    transfer(
        w_mid.at[mid_rows], ws_mid.at[0, mid_rows, theirs, :], mid_first, (0,), mate
    ).wait_recv()
    mid_share("own")
    top.share("own", 0, top.own_at, 64, across)
    mix_low("own")

    for h in range(2):
        low.recv_hop("a1", h)
        low.send_hop("relay", h)
        low.send_hop("own", h)
        low.spread("first", h)
        if h == 0:
            for n in range(2):
                low.relay("own", n)
    low.relay("first", 0)
    mix_low("first")
    low.relay("first", 1)
    turn_mid("own", core)
    mid_shared("own")
    turn_mid("own", 1 - core)
    mid.spread("own", 0)
    for h in range(2):
        low.recv_hop("relay", h)
        low.spread("both", h)
        low.recv_hop("own", h)
        low.spread("second", h)
        if h == 0:
            low.relay("both", 0)
            low.relay("second", 0)
    mid.send_hop("a1", 0)
    low.relay("both", 1)
    mix_low("both")
    low.relay("second", 1)
    top.recv_hop("a1", 0)
    top.send_hop("relay", 0)
    top.send_hop("own", 0)
    top.share("first", 0, top.own_at, 64, across)
    mix_low("second")
    mid.relay("own", 0)
    mid.recv_hop("a1", 0)
    mid.send_hop("relay", 0)
    mid.send_hop("own", 0)
    mid.spread("first", 0)
    mid_share("first")
    for name in ("own", "first", "both", "second"):
        for h in range(2):
            low.arrive(name, h)
    low.finish_local()
    contract(low)

    sums[...] = acc[...].astype(BF)
    ring_start(lambda one: sums.at[:, rows_at(one * 16, 16), :], lambda d: inbox.at[d], rs_sem)
    turn_mid("first", core)
    mid_shared("second")
    turn_mid("second", 1 - core)
    mid.recv_hop("relay", 0)
    mid.spread("both", 0)
    mid_share("both")
    mid.relay("first", 0)
    ring_recv(lambda d: inbox.at[d], rs_sem)
    total = acc[:, rows_at(leg * 16, 16), :]
    for d in range(1, LEGS):
        total = total + inbox[d].astype(F32)
    block[...] = total.astype(BF)
    ops_a[core, :, rows_at(leg * 16, 16), :] = total.astype(BF)
    ring_start(
        lambda one: block, lambda d: ops_a.at[core, :, rows_at(leg * 16, 16), :], ag_sem
    )
    mid.recv_hop("own", 0)
    mid.spread("second", 0)
    mid_share("second")
    turn_mid("both", core)
    turn_mid("second", core)
    ring_recv(
        lambda d: ops_a.at[core, :, rows_at((leg - d + LEGS) % LEGS * 16, 16), :], ag_sem
    )
    op_send = transfer(ops_a.at[core], ops_a.at[core], op_sem, (0,), mate)
    op_send.start()
    mid.relay("both", 0)
    top.recv_hop("relay", 0)
    top.share("both", 0, top.own_at, 64, across)
    top.recv_hop("own", 0)
    top.share("second", 0, top.own_at, 64, across)
    for name in ("own", "first", "both", "second"):
        top.spread(name, 0)
    mid_shared("both")
    turn_mid("both", 1 - core)
    mid_shared("first")
    turn_mid("first", 1 - core)
    mid.relay("second", 0)
    low.finish()
    transfer(ops_a.at[1 - core], ops_a.at[1 - core], op_sem, (0,), mate).wait_recv()

    load_left(lambda t, rows: ops_a[0, t, rows, :], mid.n_left, mid.left_at)
    for t in range(2):
        right_t[t] = ops_a[1, t].T
    load_right(mid.slot_legs)
    mix_mid()
    for name in ("own", "first", "both", "second"):
        mid.arrive(name, 0)
    mid.finish_local()
    contract(mid)

    ring_sent(lambda one: sums.at[:, rows_at(one * 16, 16), :], rs_sem)
    sums[...] = acc[...].astype(BF)
    mate_send = transfer(sums.at[1 - core], mate_in, mate_sem, (0,), mate)
    mate_send.start()
    top_across("own")
    top_across("first")
    transfer(mate_in, mate_in, mate_sem, (0,), mate).wait_recv()
    mid_sum[...] = (acc[core] + mate_in[...].astype(F32)).astype(BF)
    ring_start(lambda one: mid_sum.at[rows_at(one * 16, 16), :], lambda d: mid_in.at[d], rs2_sem)
    own_rows = rows_at(leg * 16, 16)
    total = acc[core, own_rows, :] + mate_in[own_rows, :].astype(F32)
    top.shared("own", 1, 128 - core * 128, 128, mate)
    turn_top("own")
    top_across("both")
    ring_recv(lambda d: mid_in.at[d], rs2_sem)
    for d in range(1, LEGS):
        total = total + mid_in[d].astype(F32)
    mid_block[...] = total.astype(BF)
    ops_b[side, core, own_rows, :] = total.astype(BF)
    ring_start(lambda one: mid_block, lambda d: ops_b.at[side, core, own_rows, :], ag2_sem)
    top_across("second")
    ring_recv(
        lambda d: ops_b.at[side, core, rows_at((leg - d + LEGS) % LEGS * 16, 16), :], ag2_sem
    )
    ours = ops_b.at[side, core]
    op2_sends = [
        transfer(ours, ours, op2_sem, (0,), mate),
        transfer(ours, ours, op2_sem, (1,), across),
    ]
    for copy in op2_sends:
        copy.start()
    top.shared("both", 1, 128 - core * 128, 128, mate)
    turn_top("both")
    top.relay("own", 0)
    top.relay("first", 0)
    top.relay("both", 0)
    other = ops_b.at[1 - side, core]
    transfer(other, other, op2_sem, (1,), across).wait_recv()
    op2_sends.append(transfer(other, other, op2_sem, (2,), mate))
    op2_sends[-1].start()
    top.relay("second", 0)
    for name in ("first", "second"):
        top.shared(name, 1, 128 - core * 128, 128, mate)
        turn_top(name)
    for n, ref in ((0, ops_b.at[side, 1 - core]), (2, ops_b.at[1 - side, 1 - core])):
        transfer(ref, ref, op2_sem, (n,), mate).wait_recv()

    load_left(lambda t, rows: ops_b[0, t, rows, :], top.n_left, top.left_at)
    for t in range(2):
        right_t[t] = ops_b[1, t].T
    load_right(top.slot_legs)
    mix_top()
    for name in ("own", "first", "both", "second"):
        top.arrive(name, 0)
    top.finish_local()
    contract(top)

    for one in range(LEGS):
        for t in range(2):
            for part in range(4):
                at = part * 64 + one * 4
                wide[one, part * 8 + t * 4 : part * 8 + t * 4 + 4, :] = acc[t, at : at + 4, :]
    rows_out[...] = wide[...].astype(BF)
    ring_start(lambda one: rows_out.at[one], lambda d: rows_in.at[d], rs3_sem)
    total = wide[leg]
    ring_recv(lambda d: rows_in.at[d], rs3_sem)
    for d in range(1, LEGS):
        total = total + rows_in[d].astype(F32)
    half_sum[...] = total.reshape(2, 2, 8, BOND)
    half_sends = []
    for n in range(2):
        copy = transfer(half_sum.at[n, 1 - core], half_in.at[n], half_sem, (n,), mate)
        copy.start()
        half_sends.append(copy)
    for n in range(2):
        transfer(half_in.at[n], half_in.at[n], half_sem, (n,), mate).wait_recv()
    side_sum[...] = half_sum[1 - side, core] + half_in[1 - side]
    side_send = transfer(side_sum, side_in, quarter_sem, (0,), across)
    side_send.start()
    total = half_sum[side, core] + half_in[side]
    transfer(side_in, side_in, quarter_sem, (0,), across).wait_recv()
    total = total + side_in[...]
    for t in range(2):
        out[0, t] = total[t * 4 : t * 4 + 4]

    for level in (mid, top):
        level.finish()
    mid_out.wait_send()
    for copy in (*top_sends, op_send, mate_send, *op2_sends, *half_sends, side_send):
        copy.wait_send()
    ring_sent(lambda one: block, ag_sem)
    ring_sent(lambda one: mid_sum.at[rows_at(one * 16, 16), :], rs2_sem)
    ring_sent(lambda one: mid_block, ag2_sem)
    ring_sent(lambda one: rows_out.at[one], rs3_sem)


def on_device(tensor_low, tensor_mid, tensor_top, child_operators, term_choice):
    dma, vmem = pltpu.SemaphoreType.DMA, pltpu.VMEM

    def level_sems(halves):
        return [
            dma((2, 3, halves)),
            dma((2, 4, halves)),
            dma((2, 4, halves)),
            dma((2, 4, halves)),
            dma((4, halves)),
            dma((2, 2, 4)),
        ]

    hbm = pl.BlockSpec(memory_space=pl.ANY)
    inside = pl.BlockSpec(memory_space=pltpu.VMEM)
    return pl.pallas_call(
        kernel,
        out_shape=jax.ShapeDtypeStruct((1, 2, 4, BOND), F32),
        in_specs=[hbm, hbm, hbm, hbm, pl.BlockSpec(memory_space=pltpu.SMEM)],
        out_specs=inside,
        scratch_shapes=[
            vmem((4, 256, 16, BOND), BF),
            vmem((4, 256, 16, BOND), BF),
            vmem((4, 256, 16, BOND), BF),
            vmem((64, 256, BOND), BF),
            vmem((32, 256, BOND), BF),
            vmem((16, 256, BOND), BF),
            vmem((4, 64, 4, BOND), BF),
            vmem((16, 256, BOND), BF),
            vmem((64, 256, BOND), BF),
            vmem((8192, 128), F32),
            vmem((8192, 128), F32),
            vmem((2, 2, 256, BOND), BF),
            vmem((2, BOND, BOND), F32),
            vmem((128, BOND), BF),
            vmem((128, BOND), BF),
            vmem((2, BOND, BOND), BF),
            vmem((2, 4, BOND, BOND), BF),
            vmem((2, BOND, BOND), BF),
            vmem((LEGS, 2, 16, BOND), BF),
            vmem((2, 16, BOND), BF),
            vmem((2, 2, BOND, BOND), BF),
            vmem((BOND, BOND), BF),
            vmem((BOND, BOND), BF),
            vmem((LEGS, 16, BOND), BF),
            vmem((16, BOND), BF),
            vmem((2, 2, BOND, BOND), BF),
            *level_sems(2),
            *level_sems(1),
            *level_sems(1),
            dma((5,)),
            dma((2, 1)),
            dma((2, 3)),
            dma((2, LEGS)),
            dma((2, LEGS)),
            dma((2, 1)),
            dma((2, 1)),
            dma((2, LEGS)),
            dma((2, LEGS)),
            dma((2, 3)),
            dma((2, 2)),
            dma((2, 1)),
            dma((2, LEGS)),
            vmem((LEGS, 32, BOND), F32),
            vmem((2, 2, 8, BOND), F32),
            vmem((2, 8, BOND), F32),
            vmem((8, BOND), F32),
            vmem((8, BOND), F32),
            vmem((LEGS, 32, BOND), BF),
            vmem((LEGS, 32, BOND), BF),
        ],
        compiler_params=pltpu.CompilerParams(
            collective_id=0, has_side_effects=True, vmem_limit_bytes=67043328
        ),
    )(tensor_low[0], tensor_mid[0], tensor_top[0], child_operators[0], term_choice[0])


def solution(mesh):
    return jax.shard_map(
        on_device,
        mesh=mesh,
        in_specs=(
            P("leaf", None, "leg", None),
            P("leaf", None, "leg", None),
            P("leaf", None, "leg", None),
            P("leaf", None, None, None, None),
            P("leaf", None, None),
        ),
        out_specs=P("leaf", None, "leg", None),
        check_vma=False,
    )
```

```python
import jax
import jax.numpy as jnp
from jax import lax
from jax.experimental import pallas as pl
from jax.experimental.pallas import tpu as pltpu
from jax.sharding import PartitionSpec as P

BF, F32 = jnp.bfloat16, jnp.float32
MESH = pl.DeviceIdType.MESH
BOND = 256
LEGS = 16


def x_near(leg):
    x = leg % 4
    return leg // 4 * 4 + x + 1 - 2 * (x % 2)


def x_far(leg):
    return leg // 4 * 4 + 3 - leg % 4


def y_near(leg):
    y = leg // 4
    return (y + 1 - 2 * (y % 2)) * 4 + leg % 4


def y_far(leg):
    return (3 - leg // 4) * 4 + leg % 4


def pick(core, first, second):
    return first + (second - first) * core


def rows_at(start, size):
    return pl.ds(pl.multiple_of(start, 8), size)


class Level:
    def __init__(self, env, ws, wl, sems, own_rows, own_at, left_bits, gather, spread, halves):
        self.env, self.ws, self.wl = env, ws, wl
        self.a_sem, self.b1_sem, self.bd_sem, self.br_sem, self.loc_sem, self.share_sem = sems
        self.own_rows, self.own_at = own_rows, own_at
        self.n_left = own_rows // 4
        self.left_at = own_at + left_bits * self.n_left
        self.halves, self.part = halves, 16 // halves
        core, leg = env["core"], env["leg"]
        fx, fy = gather
        gx, gy = spread
        self.slot_legs = [leg, fx(leg), fy(leg), fx(fy(leg))]
        self.a1 = pick(core, fx(leg), fy(leg))
        self.a2 = pick(core, fy(leg), fx(leg))
        self.first, self.second = 1 + core, 2 - core
        self.b1 = lambda one: pick(core, gy(one), gx(one))
        self.b2 = lambda one: pick(core, gx(one), gy(one))
        self.leg_of = {"own": leg, "first": self.a1, "second": self.a2, "both": fx(fy(leg))}
        self.slot_of = {"own": 0, "first": self.first, "second": self.second, "both": 3}
        self.pending = []
        self.partner_at = None

    def remote(self, src, dst, sem, index, to):
        return pltpu.make_async_remote_copy(
            src_ref=src,
            dst_ref=dst,
            send_sem=sem.at[(0, *index)],
            recv_sem=sem.at[(1, *index)],
            device_id=to,
            device_id_type=MESH,
        )

    def go(self, copy):
        copy.start()
        self.pending.append(copy)

    def piece(self, slot, h):
        return self.ws.at[
            slot, rows_at(self.left_at, self.n_left), pl.ds(h * self.part, self.part), :
        ]

    def place(self, one, h):
        return self.wl.at[:, rows_at(one * 16 + h * self.part, self.part), :]

    def to(self, one):
        return (self.env["leaf"], one)

    def hop(self, kind, h, arriving):
        src = {"a1": 0, "own": 0, "relay": self.first}[kind]
        dst = {"a1": self.first, "own": self.second, "relay": 3}[kind]
        target = self.a1 if kind == "a1" else self.a2
        index = ({"a1": 0, "own": 1, "relay": 2}[kind], h)
        rows = rows_at(self.own_at, self.own_rows)
        if kind != "a1" and self.partner_at is not None:
            rows = rows_at(self.left_at if arriving else self.partner_at, self.n_left)
        columns = pl.ds(h * self.part, self.part)
        source = self.ws.at[dst if arriving else src, rows, columns, :]
        place = self.ws.at[dst, rows, columns, :]
        return self.remote(source, place, self.a_sem, index, self.to(target))

    def send_hop(self, kind, h):
        self.go(self.hop(kind, h, False))

    def recv_hop(self, kind, h):
        self.hop(kind, h, True).wait_recv()

    def spread(self, name, h):
        slot, one = self.slot_of[name], self.leg_of[name]
        piece, place, leg = self.piece(slot, h), self.place(one, h), self.env["leg"]
        self.go(self.remote(piece, place, self.b1_sem, (slot, h), self.to(self.b1(leg))))
        self.go(self.remote(piece, place, self.bd_sem, (slot, h), self.to(self.b2(leg))))
        copy = pltpu.make_async_copy(piece, place, self.loc_sem.at[slot, h])
        copy.start()
        self.pending.append(copy)

    def relay(self, name, h):
        slot, leg = self.slot_of[name], self.env["leg"]
        place = self.place(self.b1(self.leg_of[name]), h)
        self.remote(place, place, self.b1_sem, (slot, h), self.to(self.b1(leg))).wait_recv()
        self.go(self.remote(place, place, self.br_sem, (slot, h), self.to(self.b2(leg))))

    def arrive(self, name, h):
        slot, leg, one = self.slot_of[name], self.env["leg"], self.leg_of[name]
        place = self.place(self.b2(one), h)
        self.remote(place, place, self.bd_sem, (slot, h), self.to(self.b2(leg))).wait_recv()
        place = self.place(self.b2(self.b1(one)), h)
        self.remote(place, place, self.br_sem, (slot, h), self.to(self.b2(leg))).wait_recv()

    def finish(self):
        for copy in self.pending:
            if copy.is_remote:
                copy.wait_send()

    def finish_local(self):
        for copy in self.pending:
            if not copy.is_remote:
                copy.wait()

    def share(self, name, step, start, size, to):
        slot = self.slot_of[name]
        span = self.ws.at[slot, rows_at(start, size)]
        self.go(self.remote(span, span, self.share_sem, (step, slot), to))

    def shared(self, name, step, start, size, to):
        slot = self.slot_of[name]
        span = self.ws.at[slot, rows_at(start, size)]
        self.remote(span, span, self.share_sem, (step, slot), to).wait_recv()


def transfer(src, dst, sem, index, to):
    return pltpu.make_async_remote_copy(
        src_ref=src,
        dst_ref=dst,
        send_sem=sem.at[(0, *index)],
        recv_sem=sem.at[(1, *index)],
        device_id=to,
        device_id_type=MESH,
    )


def kernel(
    w_low, w_mid, w_top, bank_in, choice, out,
    ws_low, ws_mid, ws_top, wl_low, wl_mid, wl_top, top_parts, by_row_low, by_row_mid, ys_0, ys_1,
    zs, acc, l_cat, r_cat, right_t, bank, sums, inbox, block, ops_a, mate_in, mid_sum, mid_in,
    mid_block, ops_b,
    low_a, low_b1, low_bd, low_br, low_loc, low_share,
    mid_a, mid_b1, mid_bd, mid_br, mid_loc, mid_share,
    top_a, top_b1, top_bd, top_br, top_loc, top_share,
    first_sem, mid_first, top_first, mixed_sem, rs_sem, ag_sem, op_sem,
    mate_sem, rs2_sem, ag2_sem, op2_sem, half_sem, quarter_sem, rs3_sem,
    wide, half_sum, half_in, side_sum, side_in, rows_out, rows_in,
):
    leaf, leg = lax.axis_index("leaf"), lax.axis_index("leg")
    core, z = leaf % 2, leaf // 2
    side = z % 2
    x, y = leg % 4, leg // 4
    far_x, far_y = x // 2, y // 2
    near_x, near_y = (x + far_x) % 2, (y + far_y) % 2
    mate = (leaf + 1 - 2 * core, leg)
    across = (leaf + 2 - 4 * side, leg)
    cross = (leaf + 2 - 4 * side + 1 - 2 * core, leg)
    env = {"leaf": leaf, "leg": leg, "core": core}
    near, far = (x_near, y_near), (x_far, y_far)

    low = Level(
        env, ws_low, wl_low, (low_a, low_b1, low_bd, low_br, low_loc, low_share),
        256, 0, near_x + 2 * near_y, near, far, 2,
    )
    mid = Level(
        env, ws_mid, wl_mid, (mid_a, mid_b1, mid_bd, mid_br, mid_loc, mid_share),
        128, core * 128, near_x + 2 * near_y, near, far, 2,
    )
    top = Level(
        env, ws_top, wl_top, (top_a, top_b1, top_bd, top_br, top_loc, top_share),
        64, core * 128 + side * 64, near_x + 2 * near_y, near, far, 1,
    )
    low.partner_at = 64 * pick(core, near_x + 2 - 2 * near_y, 1 - near_x + 2 * near_y)
    q = side * 2 + core
    mine, theirs = rows_at(core * 8, 8), rows_at(8 - core * 8, 8)
    mid_rows, mate_rows = rows_at(core * 128, 128), rows_at(128 - core * 128, 128)

    own_low = [
        pltpu.make_async_copy(
            w_low.at[:, pl.ds(h * 8, 8), :], ws_low.at[0, :, pl.ds(h * 8, 8), :], first_sem.at[h]
        )
        for h in range(2)
    ]
    own_mid = pltpu.make_async_copy(
        w_mid.at[mid_rows], ws_mid.at[0, mid_rows, mine, :], first_sem.at[2]
    )
    own_top = pltpu.make_async_copy(
        w_top.at[rows_at(top.own_at, 64)], top_parts.at[q], first_sem.at[3]
    )
    own_bank = pltpu.make_async_copy(bank_in, bank, first_sem.at[4])
    for copy in (*own_low, own_bank, own_mid, own_top):
        copy.start()

    barrier = pltpu.get_barrier_semaphore()

    near_by = [(leaf, hop(leg)) for hop in (x_near, x_far, y_near, y_far)]
    for peer in (*near_by, mate, across, cross):
        pl.semaphore_signal(barrier, inc=1, device_id=peer, device_id_type=MESH)
    pl.semaphore_wait(barrier, len(near_by) + 3)

    for h in range(2):
        own_low[h].wait()
        low.send_hop("a1", h)
        low.send_hop("own", h)
    mid_out = transfer(
        w_mid.at[mate_rows], ws_mid.at[0, mate_rows, mine, :], mid_first, (0,), mate
    )
    mid_out.start()
    quarters = [
        ((1 - core) * 128 + side * 64, side * 2 + 1 - core, mate),
        (core * 128 + (1 - side) * 64, (1 - side) * 2 + core, across),
        ((1 - core) * 128 + (1 - side) * 64, (1 - side) * 2 + 1 - core, cross),
    ]
    top_sends = []
    for n, (start, _, peer) in enumerate(quarters):
        copy = transfer(w_top.at[rows_at(start, 64)], top_parts.at[q], top_first, (n,), peer)
        copy.start()
        top_sends.append(copy)
    for h in range(2):
        low.spread("own", h)

    def load_left(read, n_left, at, start=0):
        for t in range(2):
            l_cat[start + t * n_left : start + (t + 1) * n_left] = read(t, rows_at(at, n_left))

    def load_right(legs):
        for t in range(2):
            for slot, one in enumerate(legs):
                start = t * 64 + slot * 16
                r_cat[start : start + 16] = right_t[t, rows_at(one * 16, 16), :]

    def mix_rows(slot, s, rows, n_left):
        mixed = jnp.dot(l_cat[: 2 * n_left], rows, preferred_element_type=F32)
        span = pl.ds(slot * 16 + s, 2 * n_left, stride=64)
        ys_0[span, :] = mixed[:, :128]
        ys_1[span, :] = mixed[:, 128:]

    def mixed_at(turn, arriving):
        return by_row_mid.at[pl.ds(32 + turn * 16, 16), pl.ds(128 * arriving, 128), :]

    def mixed_copy(turn, arriving):
        source = mixed_at(turn, 1 if arriving else 0)
        return transfer(source, mixed_at(turn, 1), mixed_sem, (turn,), (leaf, low.a2))

    def mix_low(turn, name):
        slot = low.slot_of[name]

        @pl.loop(0, 16, unroll=2)
        def _(n):
            by_row_low[:, pl.ds(n * 16, 16), :] = jnp.swapaxes(ws_low[slot, pl.ds(n * 16, 16)], 0, 1)

        @pl.loop(0, 16, unroll=4)
        def _(s):
            mixed = jnp.dot(l_cat[...], by_row_low[s], preferred_element_type=F32)
            span = pl.ds(slot * 16 + s, 128, stride=64)
            ys_0[span, :] = mixed[:128, :128]
            ys_1[span, :] = mixed[:128, 128:]
            by_row_mid[32 + turn * 16 + s, :128, :] = mixed[128:].astype(BF)

    def take_low(turn, name):
        slot = low.slot_of[name]
        mixed_copy(turn, True).wait_recv()

        @pl.loop(0, 16, unroll=4)
        def _(s):
            mixed = by_row_mid[32 + turn * 16 + s, 128:, :].astype(F32)
            span = pl.ds(slot * 16 + s, 128, stride=64)
            ys_0[span, :] = mixed[:, :128]
            ys_1[span, :] = mixed[:, 128:]

    def turn_mid(name, half):
        slot = mid.slot_of[name]

        @pl.loop(0, 8, unroll=2)
        def _(n):
            rows = rows_at(half * 128 + n * 16, 16)
            by_row_mid[pl.ds(slot * 16, 16), rows, :] = jnp.swapaxes(ws_mid[slot, rows], 0, 1)

    def mix_mid():
        @pl.loop(0, 64, unroll=8)
        def _(s):
            mix_rows(0, s, by_row_mid[s], mid.n_left)

    def turn_top(name):
        slot = top.slot_of[name]

        @pl.loop(0, 16, unroll=2)
        def _(n):
            turned = jnp.swapaxes(ws_top[slot, pl.ds(n * 16, 16)], 0, 1)
            for s in range(16):
                ws_low[slot, s * 16 + n] = turned[s]

    def mix_top():
        @pl.loop(0, 64, unroll=8)
        def _(s):
            rows = ws_low[s // 16, pl.ds(s % 16 * 16, 16)]
            mix_rows(0, s, rows.reshape(256, BOND), top.n_left)

    def contract(level):
        acc[...] = jnp.zeros_like(acc)
        n_left = level.n_left

        @pl.loop(0, n_left // 4, unroll=2)
        def _(n):
            for k in range(4):
                turned = jnp.dot(
                    r_cat[...], level.wl[n * 4 + k], preferred_element_type=F32
                ).astype(BF)
                for t in range(2):
                    zs[n % 2, t, k * 64 : (k + 1) * 64] = turned[t * 64 : (t + 1) * 64]
            for t in range(2):
                span = rows_at((t * n_left + n * 4) * 64, 256)
                rows = jnp.concatenate([ys_0[span, :], ys_1[span, :]], axis=1).astype(BF)
                acc[t] += lax.dot_general(
                    zs[n % 2, t], rows, (((0,), (0,)), ((), ())), preferred_element_type=F32
                )

    def ring_start(src_of, dst_of, sem):
        @pl.loop(1, LEGS)
        def _(d):
            one = (leg + d) % LEGS
            transfer(src_of(one), dst_of(d), sem, (d,), (leaf, one)).start()

    def ring_recv(dst_of, sem):
        @pl.loop(1, LEGS)
        def _(d):
            ref = dst_of(d)
            transfer(ref, ref, sem, (d,), (leaf, (leg + d) % LEGS)).wait_recv()

    def ring_sent(src_of, sem):
        @pl.loop(1, LEGS)
        def _(d):
            one = (leg + d) % LEGS
            ref = src_of(one)
            transfer(ref, ref, sem, (d,), (leaf, one)).wait_send()

    def mid_share(name):
        mid.share(name, 0, mid.own_at, 128, mate)

    def mid_shared(name):
        mid.shared(name, 0, 128 - core * 128, 128, mate)

    def top_across(name):
        top.shared(name, 0, core * 128 + (1 - side) * 64, 64, across)
        top.share(name, 1, core * 128, 128, mate)

    own_top.wait()
    for n, (_, part, peer) in enumerate(quarters):
        transfer(
            w_top.at[rows_at(top.own_at, 64)], top_parts.at[part], top_first, (n,), peer
        ).wait_recv()

    @pl.loop(0, 4)
    def _(n):
        for part in range(4):
            wide[:, part * 4 : part * 4 + 4, :] = top_parts[part, pl.ds(n * 16, 16), :, :].astype(
                F32
            )
        ws_top[0, rows_at(top.own_at + n * 16, 16), :, :] = wide[:, :16, :].astype(BF)

    own_bank.wait()
    for start, at in ((0, low.left_at), (128, low.partner_at)):
        load_left(lambda t, rows: bank[0, choice[t, 0], rows, :], 64, at, start)
    for t in range(2):
        right_t[t] = bank[1, choice[t, 1]].T
    load_right(low.slot_legs)
    own_mid.wait()
    transfer(
        w_mid.at[mid_rows], ws_mid.at[0, mid_rows, theirs, :], mid_first, (0,), mate
    ).wait_recv()
    mid_share("own")
    top.share("own", 0, top.own_at, 64, across)
    mix_low(0, "own")
    for h in range(2):
        low.recv_hop("own", h)
        low.spread("second", h)
    low.recv_hop("a1", 0)
    low.send_hop("relay", 0)
    mixed_copy(0, False).start()
    low.spread("first", 0)
    for h in range(2):
        low.relay("own", h)
    for h in range(2):
        low.relay("second", h)
    low.recv_hop("a1", 1)
    low.send_hop("relay", 1)
    low.spread("first", 1)
    mix_low(1, "first")
    mixed_copy(1, False).start()
    low.recv_hop("relay", 0)
    low.spread("both", 0)
    low.relay("first", 0)
    low.recv_hop("relay", 1)
    low.spread("both", 1)
    for h in range(2):
        mid.send_hop("a1", h)
    low.relay("both", 0)
    low.relay("first", 1)
    take_low(0, "second")
    low.relay("both", 1)
    take_low(1, "both")
    for name in ("own", "first", "both", "second"):
        for h in range(2):
            low.arrive(name, h)
    mid.recv_hop("a1", 0)
    mid.send_hop("relay", 0)
    mid.send_hop("own", 0)
    for h in range(2):
        mid.spread("own", h)
    mid.spread("first", 0)
    for turn in range(2):
        mixed_copy(turn, False).wait_send()
    low.finish_local()
    contract(low)

    sums[...] = acc[...].astype(BF)
    ring_start(lambda one: sums.at[:, rows_at(one * 16, 16), :], lambda d: inbox.at[d], rs_sem)
    mid.recv_hop("a1", 1)
    mid.send_hop("relay", 1)
    mid.send_hop("own", 1)
    mid.spread("first", 1)
    mid_share("first")
    top.send_hop("a1", 0)
    for h in range(2):
        mid.relay("own", h)
    mid.recv_hop("relay", 0)
    mid.spread("both", 0)
    turn_mid("own", core)
    mid_shared("own")
    turn_mid("own", 1 - core)
    mid.recv_hop("own", 0)
    mid.spread("second", 0)
    mid.relay("first", 0)
    turn_mid("first", core)
    ring_recv(lambda d: inbox.at[d], rs_sem)
    total = acc[:, rows_at(leg * 16, 16), :]
    for d in range(1, LEGS):
        total = total + inbox[d].astype(F32)
    block[...] = total.astype(BF)
    ops_a[core, :, rows_at(leg * 16, 16), :] = total.astype(BF)
    ring_start(
        lambda one: block, lambda d: ops_a.at[core, :, rows_at(leg * 16, 16), :], ag_sem
    )
    top.recv_hop("a1", 0)
    top.send_hop("relay", 0)
    top.share("first", 0, top.own_at, 64, across)
    mid.relay("first", 1)
    mid_shared("second")
    turn_mid("second", 1 - core)
    mid.recv_hop("relay", 1)
    mid.spread("both", 1)
    mid_share("both")
    mid.recv_hop("own", 1)
    mid.spread("second", 1)
    mid_share("second")
    top.send_hop("own", 0)
    mid.relay("both", 0)
    mid.relay("second", 0)
    turn_mid("both", core)
    turn_mid("second", core)
    for name in ("both", "second"):
        mid.relay(name, 1)
    ring_recv(
        lambda d: ops_a.at[core, :, rows_at((leg - d + LEGS) % LEGS * 16, 16), :], ag_sem
    )
    op_send = transfer(ops_a.at[core], ops_a.at[core], op_sem, (0,), mate)
    op_send.start()
    top.recv_hop("relay", 0)
    top.share("both", 0, top.own_at, 64, across)
    for name in ("own", "first"):
        top.spread(name, 0)
    mid_shared("both")
    turn_mid("both", 1 - core)
    mid_shared("first")
    turn_mid("first", 1 - core)
    low.finish()
    transfer(ops_a.at[1 - core], ops_a.at[1 - core], op_sem, (0,), mate).wait_recv()

    load_left(lambda t, rows: ops_a[0, t, rows, :], mid.n_left, mid.left_at)
    for t in range(2):
        right_t[t] = ops_a[1, t].T
    load_right(mid.slot_legs)
    mix_mid()
    top.recv_hop("own", 0)
    top.share("second", 0, top.own_at, 64, across)
    for name in ("both", "second"):
        top.spread(name, 0)
    for name in ("own", "first", "both", "second"):
        for h in range(2):
            mid.arrive(name, h)
    mid.finish_local()
    contract(mid)

    ring_sent(lambda one: sums.at[:, rows_at(one * 16, 16), :], rs_sem)
    sums[...] = acc[...].astype(BF)
    mate_send = transfer(sums.at[1 - core], mate_in, mate_sem, (0,), mate)
    mate_send.start()
    top_across("own")
    top_across("first")
    transfer(mate_in, mate_in, mate_sem, (0,), mate).wait_recv()
    mid_sum[...] = (acc[core] + mate_in[...].astype(F32)).astype(BF)
    ring_start(lambda one: mid_sum.at[rows_at(one * 16, 16), :], lambda d: mid_in.at[d], rs2_sem)
    own_rows = rows_at(leg * 16, 16)
    total = acc[core, own_rows, :] + mate_in[own_rows, :].astype(F32)
    top.shared("own", 1, 128 - core * 128, 128, mate)
    turn_top("own")
    top_across("both")
    ring_recv(lambda d: mid_in.at[d], rs2_sem)
    for d in range(1, LEGS):
        total = total + mid_in[d].astype(F32)
    mid_block[...] = total.astype(BF)
    ops_b[side, core, own_rows, :] = total.astype(BF)
    ring_start(lambda one: mid_block, lambda d: ops_b.at[side, core, own_rows, :], ag2_sem)
    top_across("second")
    ring_recv(
        lambda d: ops_b.at[side, core, rows_at((leg - d + LEGS) % LEGS * 16, 16), :], ag2_sem
    )
    ours = ops_b.at[side, core]
    op2_sends = [
        transfer(ours, ours, op2_sem, (0,), mate),
        transfer(ours, ours, op2_sem, (1,), across),
    ]
    for copy in op2_sends:
        copy.start()
    top.shared("both", 1, 128 - core * 128, 128, mate)
    turn_top("both")
    top.relay("own", 0)
    top.relay("first", 0)
    top.relay("both", 0)
    other = ops_b.at[1 - side, core]
    transfer(other, other, op2_sem, (1,), across).wait_recv()
    op2_sends.append(transfer(other, other, op2_sem, (2,), mate))
    op2_sends[-1].start()
    top.relay("second", 0)
    for name in ("first", "second"):
        top.shared(name, 1, 128 - core * 128, 128, mate)
        turn_top(name)
    for n, ref in ((0, ops_b.at[side, 1 - core]), (2, ops_b.at[1 - side, 1 - core])):
        transfer(ref, ref, op2_sem, (n,), mate).wait_recv()

    load_left(lambda t, rows: ops_b[0, t, rows, :], top.n_left, top.left_at)
    for t in range(2):
        right_t[t] = ops_b[1, t].T
    load_right(top.slot_legs)
    mix_top()
    for name in ("own", "first", "both", "second"):
        top.arrive(name, 0)
    top.finish_local()
    contract(top)

    for one in range(LEGS):
        for t in range(2):
            for part in range(4):
                at = part * 64 + one * 4
                wide[one, part * 8 + t * 4 : part * 8 + t * 4 + 4, :] = acc[t, at : at + 4, :]
    rows_out[...] = wide[...].astype(BF)
    ring_start(lambda one: rows_out.at[one], lambda d: rows_in.at[d], rs3_sem)
    total = wide[leg]
    ring_recv(lambda d: rows_in.at[d], rs3_sem)
    for d in range(1, LEGS):
        total = total + rows_in[d].astype(F32)
    half_sum[...] = total.reshape(2, 2, 8, BOND)
    half_sends = []
    for n in range(2):
        copy = transfer(half_sum.at[n, 1 - core], half_in.at[n], half_sem, (n,), mate)
        copy.start()
        half_sends.append(copy)
    for n in range(2):
        transfer(half_in.at[n], half_in.at[n], half_sem, (n,), mate).wait_recv()
    side_sum[...] = half_sum[1 - side, core] + half_in[1 - side]
    side_send = transfer(side_sum, side_in, quarter_sem, (0,), across)
    side_send.start()
    total = half_sum[side, core] + half_in[side]
    transfer(side_in, side_in, quarter_sem, (0,), across).wait_recv()
    total = total + side_in[...]
    for t in range(2):
        out[0, t] = total[t * 4 : t * 4 + 4]

    for level in (mid, top):
        level.finish()
    mid_out.wait_send()
    for copy in (*top_sends, op_send, mate_send, *op2_sends, *half_sends, side_send):
        copy.wait_send()
    ring_sent(lambda one: block, ag_sem)
    ring_sent(lambda one: mid_sum.at[rows_at(one * 16, 16), :], rs2_sem)
    ring_sent(lambda one: mid_block, ag2_sem)
    ring_sent(lambda one: rows_out.at[one], rs3_sem)


def on_device(tensor_low, tensor_mid, tensor_top, child_operators, term_choice):
    dma, vmem = pltpu.SemaphoreType.DMA, pltpu.VMEM

    def level_sems(halves):
        return [
            dma((2, 3, halves)),
            dma((2, 4, halves)),
            dma((2, 4, halves)),
            dma((2, 4, halves)),
            dma((4, halves)),
            dma((2, 2, 4)),
        ]

    hbm = pl.BlockSpec(memory_space=pl.ANY)
    inside = pl.BlockSpec(memory_space=pltpu.VMEM)
    return pl.pallas_call(
        kernel,
        out_shape=jax.ShapeDtypeStruct((1, 2, 4, BOND), F32),
        in_specs=[hbm, hbm, hbm, hbm, pl.BlockSpec(memory_space=pltpu.SMEM)],
        out_specs=inside,
        scratch_shapes=[
            vmem((4, 256, 16, BOND), BF),
            vmem((4, 256, 16, BOND), BF),
            vmem((4, 256, 16, BOND), BF),
            vmem((64, 256, BOND), BF),
            vmem((32, 256, BOND), BF),
            vmem((16, 256, BOND), BF),
            vmem((4, 64, 4, BOND), BF),
            vmem((16, 256, BOND), BF),
            vmem((64, 256, BOND), BF),
            vmem((8192, 128), F32),
            vmem((8192, 128), F32),
            vmem((2, 2, 256, BOND), BF),
            vmem((2, BOND, BOND), F32),
            vmem((256, BOND), BF),
            vmem((128, BOND), BF),
            vmem((2, BOND, BOND), BF),
            vmem((2, 4, BOND, BOND), BF),
            vmem((2, BOND, BOND), BF),
            vmem((LEGS, 2, 16, BOND), BF),
            vmem((2, 16, BOND), BF),
            vmem((2, 2, BOND, BOND), BF),
            vmem((BOND, BOND), BF),
            vmem((BOND, BOND), BF),
            vmem((LEGS, 16, BOND), BF),
            vmem((16, BOND), BF),
            vmem((2, 2, BOND, BOND), BF),
            *level_sems(2),
            *level_sems(2),
            *level_sems(1),
            dma((5,)),
            dma((2, 1)),
            dma((2, 3)),
            dma((2, 2)),
            dma((2, LEGS)),
            dma((2, LEGS)),
            dma((2, 1)),
            dma((2, 1)),
            dma((2, LEGS)),
            dma((2, LEGS)),
            dma((2, 3)),
            dma((2, 2)),
            dma((2, 1)),
            dma((2, LEGS)),
            vmem((LEGS, 32, BOND), F32),
            vmem((2, 2, 8, BOND), F32),
            vmem((2, 8, BOND), F32),
            vmem((8, BOND), F32),
            vmem((8, BOND), F32),
            vmem((LEGS, 32, BOND), BF),
            vmem((LEGS, 32, BOND), BF),
        ],
        compiler_params=pltpu.CompilerParams(
            collective_id=0, has_side_effects=True, vmem_limit_bytes=67043328
        ),
    )(tensor_low[0], tensor_mid[0], tensor_top[0], child_operators[0], term_choice[0])


def solution(mesh):
    return jax.shard_map(
        on_device,
        mesh=mesh,
        in_specs=(
            P("leaf", None, "leg", None),
            P("leaf", None, "leg", None),
            P("leaf", None, "leg", None),
            P("leaf", None, None, None, None),
            P("leaf", None, None),
        ),
        out_specs=P("leaf", None, "leg", None),
        check_vma=False,
    )
```

```python
import jax
import jax.numpy as jnp
from jax import lax
from jax.experimental import pallas as pl
from jax.experimental.pallas import tpu as pltpu
from jax.sharding import PartitionSpec as P

BF, F32 = jnp.bfloat16, jnp.float32
MESH = pl.DeviceIdType.MESH
BOND = 256
LEGS = 16


def x_near(leg):
    x = leg % 4
    return leg // 4 * 4 + x + 1 - 2 * (x % 2)


def x_far(leg):
    return leg // 4 * 4 + 3 - leg % 4


def y_near(leg):
    y = leg // 4
    return (y + 1 - 2 * (y % 2)) * 4 + leg % 4


def y_far(leg):
    return (3 - leg // 4) * 4 + leg % 4


def pick(core, first, second):
    return first + (second - first) * core


def rows_at(start, size):
    return pl.ds(pl.multiple_of(start, 8), size)


class Level:
    def __init__(self, env, ws, wl, sems, own_rows, own_at, left_bits, gather, spread, halves):
        self.env, self.ws, self.wl = env, ws, wl
        self.a_sem, self.b1_sem, self.bd_sem, self.br_sem, self.loc_sem, self.share_sem = sems
        self.own_rows, self.own_at = own_rows, own_at
        self.n_left = own_rows // 4
        self.left_at = own_at + left_bits * self.n_left
        self.halves, self.part = halves, 16 // halves
        core, leg = env["core"], env["leg"]
        fx, fy = gather
        gx, gy = spread
        self.slot_legs = [leg, fx(leg), fy(leg), fx(fy(leg))]
        self.a1 = pick(core, fx(leg), fy(leg))
        self.a2 = pick(core, fy(leg), fx(leg))
        self.first, self.second = 1 + core, 2 - core
        self.b1 = lambda one: pick(core, gy(one), gx(one))
        self.b2 = lambda one: pick(core, gx(one), gy(one))
        self.leg_of = {"own": leg, "first": self.a1, "second": self.a2, "both": fx(fy(leg))}
        self.slot_of = {"own": 0, "first": self.first, "second": self.second, "both": 3}
        self.pending = []
        self.partner_at = None

    def remote(self, src, dst, sem, index, to):
        return pltpu.make_async_remote_copy(
            src_ref=src,
            dst_ref=dst,
            send_sem=sem.at[(0, *index)],
            recv_sem=sem.at[(1, *index)],
            device_id=to,
            device_id_type=MESH,
        )

    def go(self, copy):
        copy.start()
        self.pending.append(copy)

    def piece(self, slot, h):
        return self.ws.at[
            slot, rows_at(self.left_at, self.n_left), pl.ds(h * self.part, self.part), :
        ]

    def place(self, one, h):
        return self.wl.at[:, rows_at(one * 16 + h * self.part, self.part), :]

    def to(self, one):
        return (self.env["leaf"], one)

    def hop(self, kind, h, arriving):
        src = {"a1": 0, "own": 0, "relay": self.first}[kind]
        dst = {"a1": self.first, "own": self.second, "relay": 3}[kind]
        target = self.a1 if kind == "a1" else self.a2
        index = ({"a1": 0, "own": 1, "relay": 2}[kind], h)
        rows = rows_at(self.own_at, self.own_rows)
        if kind != "a1" and self.partner_at is not None:
            rows = rows_at(self.left_at if arriving else self.partner_at, self.n_left)
        columns = pl.ds(h * self.part, self.part)
        source = self.ws.at[dst if arriving else src, rows, columns, :]
        place = self.ws.at[dst, rows, columns, :]
        return self.remote(source, place, self.a_sem, index, self.to(target))

    def send_hop(self, kind, h):
        self.go(self.hop(kind, h, False))

    def recv_hop(self, kind, h):
        self.hop(kind, h, True).wait_recv()

    def spread(self, name, h):
        slot, one = self.slot_of[name], self.leg_of[name]
        piece, place, leg = self.piece(slot, h), self.place(one, h), self.env["leg"]
        self.go(self.remote(piece, place, self.b1_sem, (slot, h), self.to(self.b1(leg))))
        self.go(self.remote(piece, place, self.bd_sem, (slot, h), self.to(self.b2(leg))))
        copy = pltpu.make_async_copy(piece, place, self.loc_sem.at[slot, h])
        copy.start()
        self.pending.append(copy)

    def relay(self, name, h):
        slot, leg = self.slot_of[name], self.env["leg"]
        place = self.place(self.b1(self.leg_of[name]), h)
        self.remote(place, place, self.b1_sem, (slot, h), self.to(self.b1(leg))).wait_recv()
        self.go(self.remote(place, place, self.br_sem, (slot, h), self.to(self.b2(leg))))

    def arrive(self, name, h):
        slot, leg, one = self.slot_of[name], self.env["leg"], self.leg_of[name]
        place = self.place(self.b2(one), h)
        self.remote(place, place, self.bd_sem, (slot, h), self.to(self.b2(leg))).wait_recv()
        place = self.place(self.b2(self.b1(one)), h)
        self.remote(place, place, self.br_sem, (slot, h), self.to(self.b2(leg))).wait_recv()

    def finish(self):
        for copy in self.pending:
            if copy.is_remote:
                copy.wait_send()

    def finish_local(self):
        for copy in self.pending:
            if not copy.is_remote:
                copy.wait()

    def share(self, name, step, start, size, to):
        slot = self.slot_of[name]
        span = self.ws.at[slot, rows_at(start, size)]
        self.go(self.remote(span, span, self.share_sem, (step, slot), to))

    def shared(self, name, step, start, size, to):
        slot = self.slot_of[name]
        span = self.ws.at[slot, rows_at(start, size)]
        self.remote(span, span, self.share_sem, (step, slot), to).wait_recv()


def transfer(src, dst, sem, index, to):
    return pltpu.make_async_remote_copy(
        src_ref=src,
        dst_ref=dst,
        send_sem=sem.at[(0, *index)],
        recv_sem=sem.at[(1, *index)],
        device_id=to,
        device_id_type=MESH,
    )


def kernel(
    w_low, w_mid, w_top, bank_in, choice, out,
    ws_low, ws_mid, ws_top, wl_low, wl_mid, wl_top, top_parts, by_row_low, by_row_mid, ys_0, ys_1,
    zs, acc, l_cat, r_cat, right_t, bank, sums, inbox, block, ops_a, mate_in, mid_sum, mid_in,
    mid_block, ops_b,
    low_a, low_b1, low_bd, low_br, low_loc, low_share,
    mid_a, mid_b1, mid_bd, mid_br, mid_loc, mid_share,
    top_a, top_b1, top_bd, top_br, top_loc, top_share,
    first_sem, mid_first, top_first, mixed_sem, rs_sem, ag_sem, op_sem,
    mate_sem, rs2_sem, ag2_sem, op2_sem, half_sem, quarter_sem, rs3_sem,
    wide, half_sum, half_in, side_sum, side_in, rows_out, rows_in,
):
    leaf, leg = lax.axis_index("leaf"), lax.axis_index("leg")
    core, z = leaf % 2, leaf // 2
    side = z % 2
    x, y = leg % 4, leg // 4
    far_x, far_y = x // 2, y // 2
    near_x, near_y = (x + far_x) % 2, (y + far_y) % 2
    mate = (leaf + 1 - 2 * core, leg)
    across = (leaf + 2 - 4 * side, leg)
    cross = (leaf + 2 - 4 * side + 1 - 2 * core, leg)
    env = {"leaf": leaf, "leg": leg, "core": core}
    near, far = (x_near, y_near), (x_far, y_far)

    low = Level(
        env, ws_low, wl_low, (low_a, low_b1, low_bd, low_br, low_loc, low_share),
        256, 0, near_x + 2 * near_y, near, far, 2,
    )
    mid = Level(
        env, ws_mid, wl_mid, (mid_a, mid_b1, mid_bd, mid_br, mid_loc, mid_share),
        128, core * 128, near_x + 2 * near_y, near, far, 2,
    )
    top = Level(
        env, ws_top, wl_top, (top_a, top_b1, top_bd, top_br, top_loc, top_share),
        64, core * 128 + side * 64, near_x + 2 * near_y, near, far, 1,
    )
    low.partner_at = 64 * pick(core, near_x + 2 - 2 * near_y, 1 - near_x + 2 * near_y)
    q = side * 2 + core
    mine, theirs = rows_at(core * 8, 8), rows_at(8 - core * 8, 8)
    mid_rows, mate_rows = rows_at(core * 128, 128), rows_at(128 - core * 128, 128)

    own_low = [
        pltpu.make_async_copy(
            w_low.at[:, pl.ds(h * 8, 8), :], ws_low.at[0, :, pl.ds(h * 8, 8), :], first_sem.at[h]
        )
        for h in range(2)
    ]
    own_mid = pltpu.make_async_copy(
        w_mid.at[mid_rows], ws_mid.at[0, mid_rows, mine, :], first_sem.at[2]
    )
    own_top = pltpu.make_async_copy(
        w_top.at[rows_at(top.own_at, 64)], top_parts.at[q], first_sem.at[3]
    )
    own_bank = pltpu.make_async_copy(bank_in, bank, first_sem.at[4])
    for copy in (*own_low, own_bank, own_mid, own_top):
        copy.start()

    barrier = pltpu.get_barrier_semaphore()

    near_by = [(leaf, hop(leg)) for hop in (x_near, x_far, y_near, y_far)]
    for peer in (*near_by, mate, across, cross):
        pl.semaphore_signal(barrier, inc=1, device_id=peer, device_id_type=MESH)
    pl.semaphore_wait(barrier, len(near_by) + 3)

    for h in range(2):
        own_low[h].wait()
        low.send_hop("a1", h)
        low.send_hop("own", h)
    mid_out = transfer(
        w_mid.at[mate_rows], ws_mid.at[0, mate_rows, mine, :], mid_first, (0,), mate
    )
    mid_out.start()
    quarters = [
        ((1 - core) * 128 + side * 64, side * 2 + 1 - core, mate),
        (core * 128 + (1 - side) * 64, (1 - side) * 2 + core, across),
        ((1 - core) * 128 + (1 - side) * 64, (1 - side) * 2 + 1 - core, cross),
    ]
    top_sends = []
    for n, (start, _, peer) in enumerate(quarters):
        copy = transfer(w_top.at[rows_at(start, 64)], top_parts.at[q], top_first, (n,), peer)
        copy.start()
        top_sends.append(copy)
    for h in range(2):
        low.spread("own", h)

    def load_left(read, n_left, at, start=0):
        for t in range(2):
            l_cat[start + t * n_left : start + (t + 1) * n_left] = read(t, rows_at(at, n_left))

    def load_right(legs):
        for t in range(2):
            for slot, one in enumerate(legs):
                start = t * 64 + slot * 16
                r_cat[start : start + 16] = right_t[t, rows_at(one * 16, 16), :]

    def mix_rows(slot, s, rows, n_left):
        mixed = jnp.dot(l_cat[: 2 * n_left], rows, preferred_element_type=F32)
        span = pl.ds(slot * 16 + s, 2 * n_left, stride=64)
        ys_0[span, :] = mixed[:, :128]
        ys_1[span, :] = mixed[:, 128:]

    def mixed_at(turn, arriving):
        return by_row_mid.at[pl.ds(32 + turn * 16, 16), pl.ds(128 * arriving, 128), :]

    def mixed_copy(turn, arriving):
        source = mixed_at(turn, 1 if arriving else 0)
        return transfer(source, mixed_at(turn, 1), mixed_sem, (turn,), (leaf, low.a2))

    def mix_low(turn, name):
        slot = low.slot_of[name]

        @pl.loop(0, 16, unroll=2)
        def _(n):
            by_row_low[:, pl.ds(n * 16, 16), :] = jnp.swapaxes(ws_low[slot, pl.ds(n * 16, 16)], 0, 1)

        @pl.loop(0, 16, unroll=4)
        def _(s):
            mixed = jnp.dot(l_cat[...], by_row_low[s], preferred_element_type=F32)
            span = pl.ds(slot * 16 + s, 128, stride=64)
            ys_0[span, :] = mixed[:128, :128]
            ys_1[span, :] = mixed[:128, 128:]
            by_row_mid[32 + turn * 16 + s, :128, :] = mixed[128:].astype(BF)

    def take_low(turn, name):
        slot = low.slot_of[name]
        mixed_copy(turn, True).wait_recv()

        @pl.loop(0, 16, unroll=4)
        def _(s):
            mixed = by_row_mid[32 + turn * 16 + s, 128:, :].astype(F32)
            span = pl.ds(slot * 16 + s, 128, stride=64)
            ys_0[span, :] = mixed[:, :128]
            ys_1[span, :] = mixed[:, 128:]

    def turn_mid(name, half):
        slot = mid.slot_of[name]

        @pl.loop(0, 8, unroll=2)
        def _(n):
            rows = rows_at(half * 128 + n * 16, 16)
            by_row_mid[pl.ds(slot * 16, 16), rows, :] = jnp.swapaxes(ws_mid[slot, rows], 0, 1)

    def mix_mid():
        @pl.loop(0, 64, unroll=8)
        def _(s):
            mix_rows(0, s, by_row_mid[s], mid.n_left)

    def turn_top(name, half):
        slot = top.slot_of[name]

        @pl.loop(0, 8, unroll=2)
        def _(n):
            at = half * 8 + n
            turned = jnp.swapaxes(ws_top[slot, rows_at(at * 16, 16)], 0, 1)
            for s in range(16):
                ws_low[slot, s * 16 + at] = turned[s]

    def mix_top(name):
        slot = top.slot_of[name]

        @pl.loop(0, 16, unroll=8)
        def _(s):
            rows = ws_low[slot, pl.ds(s * 16, 16)]
            mix_rows(slot, s, rows.reshape(256, BOND), top.n_left)

    def contract(level):
        acc[...] = jnp.zeros_like(acc)
        n_left = level.n_left

        @pl.loop(0, n_left // 4, unroll=2)
        def _(n):
            for k in range(4):
                turned = jnp.dot(
                    r_cat[...], level.wl[n * 4 + k], preferred_element_type=F32
                ).astype(BF)
                for t in range(2):
                    zs[n % 2, t, k * 64 : (k + 1) * 64] = turned[t * 64 : (t + 1) * 64]
            for t in range(2):
                span = rows_at((t * n_left + n * 4) * 64, 256)
                rows = jnp.concatenate([ys_0[span, :], ys_1[span, :]], axis=1).astype(BF)
                acc[t] += lax.dot_general(
                    zs[n % 2, t], rows, (((0,), (0,)), ((), ())), preferred_element_type=F32
                )

    def ring_start(src_of, dst_of, sem):
        @pl.loop(1, LEGS)
        def _(d):
            one = (leg + d) % LEGS
            transfer(src_of(one), dst_of(d), sem, (d,), (leaf, one)).start()

    def ring_recv(dst_of, sem):
        @pl.loop(1, LEGS)
        def _(d):
            ref = dst_of(d)
            transfer(ref, ref, sem, (d,), (leaf, (leg + d) % LEGS)).wait_recv()

    def ring_sent(src_of, sem):
        @pl.loop(1, LEGS)
        def _(d):
            one = (leg + d) % LEGS
            ref = src_of(one)
            transfer(ref, ref, sem, (d,), (leaf, one)).wait_send()

    def mid_share(name):
        mid.share(name, 0, mid.own_at, 128, mate)

    def mid_shared(name):
        mid.shared(name, 0, 128 - core * 128, 128, mate)

    def top_shared(name):
        top.shared(name, 1, 128 - core * 128, 128, mate)

    def top_across(name):
        top.shared(name, 0, core * 128 + (1 - side) * 64, 64, across)
        top.share(name, 1, core * 128, 128, mate)

    own_top.wait()
    for n, (_, part, peer) in enumerate(quarters):
        transfer(
            w_top.at[rows_at(top.own_at, 64)], top_parts.at[part], top_first, (n,), peer
        ).wait_recv()

    @pl.loop(0, 4)
    def _(n):
        for part in range(4):
            wide[:, part * 4 : part * 4 + 4, :] = top_parts[part, pl.ds(n * 16, 16), :, :].astype(
                F32
            )
        ws_top[0, rows_at(top.own_at + n * 16, 16), :, :] = wide[:, :16, :].astype(BF)

    own_bank.wait()
    for start, at in ((0, low.left_at), (128, low.partner_at)):
        load_left(lambda t, rows: bank[0, choice[t, 0], rows, :], 64, at, start)
    for t in range(2):
        right_t[t] = bank[1, choice[t, 1]].T
    load_right(low.slot_legs)
    own_mid.wait()
    transfer(
        w_mid.at[mid_rows], ws_mid.at[0, mid_rows, theirs, :], mid_first, (0,), mate
    ).wait_recv()
    mid_share("own")
    top.share("own", 0, top.own_at, 64, across)
    mix_low(0, "own")
    for h in range(2):
        low.recv_hop("own", h)
        low.spread("second", h)
    low.recv_hop("a1", 0)
    low.send_hop("relay", 0)
    mixed_copy(0, False).start()
    low.spread("first", 0)
    for h in range(2):
        low.relay("own", h)
    for h in range(2):
        low.relay("second", h)
    low.recv_hop("a1", 1)
    low.send_hop("relay", 1)
    low.spread("first", 1)
    mix_low(1, "first")
    mixed_copy(1, False).start()
    low.recv_hop("relay", 0)
    low.spread("both", 0)
    low.relay("first", 0)
    low.recv_hop("relay", 1)
    low.spread("both", 1)
    for h in range(2):
        mid.send_hop("a1", h)
    low.relay("both", 0)
    low.relay("first", 1)
    take_low(0, "second")
    low.relay("both", 1)
    take_low(1, "both")
    for name in ("own", "first", "both", "second"):
        for h in range(2):
            low.arrive(name, h)
    mid.recv_hop("a1", 0)
    mid.send_hop("relay", 0)
    mid.send_hop("own", 0)
    for h in range(2):
        mid.spread("own", h)
    mid.spread("first", 0)
    top_across("own")
    for turn in range(2):
        mixed_copy(turn, False).wait_send()
    low.finish_local()
    contract(low)

    sums[...] = acc[...].astype(BF)
    ring_start(lambda one: sums.at[:, rows_at(one * 16, 16), :], lambda d: inbox.at[d], rs_sem)
    mid.recv_hop("a1", 1)
    mid.send_hop("relay", 1)
    mid.send_hop("own", 1)
    mid.spread("first", 1)
    mid_share("first")
    top.send_hop("a1", 0)
    for h in range(2):
        mid.relay("own", h)
    mid.recv_hop("relay", 0)
    mid.spread("both", 0)
    turn_mid("own", core)
    mid_shared("own")
    turn_mid("own", 1 - core)
    mid.recv_hop("own", 0)
    mid.spread("second", 0)
    mid.relay("first", 0)
    turn_mid("first", core)
    ring_recv(lambda d: inbox.at[d], rs_sem)
    total = acc[:, rows_at(leg * 16, 16), :]
    for d in range(1, LEGS):
        total = total + inbox[d].astype(F32)
    block[...] = total.astype(BF)
    ops_a[core, :, rows_at(leg * 16, 16), :] = total.astype(BF)
    ring_start(
        lambda one: block, lambda d: ops_a.at[core, :, rows_at(leg * 16, 16), :], ag_sem
    )
    top.recv_hop("a1", 0)
    top.send_hop("relay", 0)
    top.share("first", 0, top.own_at, 64, across)
    mid.relay("first", 1)
    mid_shared("second")
    turn_mid("second", 1 - core)
    mid.recv_hop("relay", 1)
    mid.spread("both", 1)
    mid_share("both")
    mid.recv_hop("own", 1)
    mid.spread("second", 1)
    mid_share("second")
    top.send_hop("own", 0)
    mid.relay("both", 0)
    mid.relay("second", 0)
    turn_mid("both", core)
    turn_mid("second", core)
    mid.relay("both", 1)
    ring_recv(
        lambda d: ops_a.at[core, :, rows_at((leg - d + LEGS) % LEGS * 16, 16), :], ag_sem
    )
    op_send = transfer(ops_a.at[core], ops_a.at[core], op_sem, (0,), mate)
    op_send.start()
    mid_shared("both")
    turn_mid("both", 1 - core)
    mid_shared("first")
    turn_mid("first", 1 - core)
    top_across("first")
    low.finish()
    transfer(ops_a.at[1 - core], ops_a.at[1 - core], op_sem, (0,), mate).wait_recv()

    load_left(lambda t, rows: ops_a[0, t, rows, :], mid.n_left, mid.left_at)
    for t in range(2):
        right_t[t] = ops_a[1, t].T
    load_right(mid.slot_legs)
    mix_mid()
    mid.relay("second", 1)
    top.recv_hop("relay", 0)
    top.share("both", 0, top.own_at, 64, across)
    for name in ("own", "first"):
        top.spread(name, 0)
    top.recv_hop("own", 0)
    top.share("second", 0, top.own_at, 64, across)
    for name in ("both", "second"):
        top.spread(name, 0)
    top_shared("own")
    for half in range(2):
        turn_top("own", half)
    for name in ("own", "first", "both", "second"):
        for h in range(2):
            mid.arrive(name, h)
    mid.finish_local()
    contract(mid)

    ring_sent(lambda one: sums.at[:, rows_at(one * 16, 16), :], rs_sem)
    sums[...] = acc[...].astype(BF)
    mate_send = transfer(sums.at[1 - core], mate_in, mate_sem, (0,), mate)
    mate_send.start()
    transfer(mate_in, mate_in, mate_sem, (0,), mate).wait_recv()
    mid_sum[...] = (acc[core] + mate_in[...].astype(F32)).astype(BF)
    ring_start(lambda one: mid_sum.at[rows_at(one * 16, 16), :], lambda d: mid_in.at[d], rs2_sem)
    own_rows = rows_at(leg * 16, 16)
    total = acc[core, own_rows, :] + mate_in[own_rows, :].astype(F32)
    top_shared("second")
    turn_top("second", 1 - core)
    turn_top("first", core)
    ring_recv(lambda d: mid_in.at[d], rs2_sem)
    for d in range(1, LEGS):
        total = total + mid_in[d].astype(F32)
    mid_block[...] = total.astype(BF)
    ops_b[side, core, own_rows, :] = total.astype(BF)
    ring_start(lambda one: mid_block, lambda d: ops_b.at[side, core, own_rows, :], ag2_sem)
    top.relay("own", 0)
    top.relay("first", 0)
    top_across("both")
    turn_top("both", core)
    ring_recv(
        lambda d: ops_b.at[side, core, rows_at((leg - d + LEGS) % LEGS * 16, 16), :], ag2_sem
    )
    ours = ops_b.at[side, core]
    op2_sends = [
        transfer(ours, ours, op2_sem, (0,), mate),
        transfer(ours, ours, op2_sem, (1,), across),
    ]
    for copy in op2_sends:
        copy.start()
    top_shared("both")
    turn_top("both", 1 - core)
    top_across("second")
    turn_top("second", core)
    top.relay("both", 0)
    top.relay("second", 0)
    other = ops_b.at[1 - side, core]
    transfer(other, other, op2_sem, (1,), across).wait_recv()
    op2_sends.append(transfer(other, other, op2_sem, (2,), mate))
    op2_sends[-1].start()
    for n, ref in ((0, ops_b.at[side, 1 - core]), (2, ops_b.at[1 - side, 1 - core])):
        transfer(ref, ref, op2_sem, (n,), mate).wait_recv()

    load_left(lambda t, rows: ops_b[0, t, rows, :], top.n_left, top.left_at)
    for t in range(2):
        right_t[t] = ops_b[1, t].T
    load_right(top.slot_legs)
    mix_top("own")
    mix_top("both")
    top_shared("first")
    turn_top("first", 1 - core)
    mix_top("first")
    mix_top("second")
    for name in ("own", "first", "both", "second"):
        top.arrive(name, 0)
    top.finish_local()
    contract(top)

    for one in range(LEGS):
        for t in range(2):
            for part in range(4):
                at = part * 64 + one * 4
                wide[one, part * 8 + t * 4 : part * 8 + t * 4 + 4, :] = acc[t, at : at + 4, :]
    rows_out[...] = wide[...].astype(BF)
    ring_start(lambda one: rows_out.at[one], lambda d: rows_in.at[d], rs3_sem)
    total = wide[leg]
    ring_recv(lambda d: rows_in.at[d], rs3_sem)
    for d in range(1, LEGS):
        total = total + rows_in[d].astype(F32)
    half_sum[...] = total.reshape(2, 2, 8, BOND)
    half_sends = []
    for n in range(2):
        copy = transfer(half_sum.at[n, 1 - core], half_in.at[n], half_sem, (n,), mate)
        copy.start()
        half_sends.append(copy)
    for n in range(2):
        transfer(half_in.at[n], half_in.at[n], half_sem, (n,), mate).wait_recv()
    side_sum[...] = half_sum[1 - side, core] + half_in[1 - side]
    side_send = transfer(side_sum, side_in, quarter_sem, (0,), across)
    side_send.start()
    total = half_sum[side, core] + half_in[side]
    transfer(side_in, side_in, quarter_sem, (0,), across).wait_recv()
    total = total + side_in[...]
    for t in range(2):
        out[0, t] = total[t * 4 : t * 4 + 4]

    for level in (mid, top):
        level.finish()
    mid_out.wait_send()
    for copy in (*top_sends, op_send, mate_send, *op2_sends, *half_sends, side_send):
        copy.wait_send()
    ring_sent(lambda one: block, ag_sem)
    ring_sent(lambda one: mid_sum.at[rows_at(one * 16, 16), :], rs2_sem)
    ring_sent(lambda one: mid_block, ag2_sem)
    ring_sent(lambda one: rows_out.at[one], rs3_sem)


def on_device(tensor_low, tensor_mid, tensor_top, child_operators, term_choice):
    dma, vmem = pltpu.SemaphoreType.DMA, pltpu.VMEM

    def level_sems(halves):
        return [
            dma((2, 3, halves)),
            dma((2, 4, halves)),
            dma((2, 4, halves)),
            dma((2, 4, halves)),
            dma((4, halves)),
            dma((2, 2, 4)),
        ]

    hbm = pl.BlockSpec(memory_space=pl.ANY)
    inside = pl.BlockSpec(memory_space=pltpu.VMEM)
    return pl.pallas_call(
        kernel,
        out_shape=jax.ShapeDtypeStruct((1, 2, 4, BOND), F32),
        in_specs=[hbm, hbm, hbm, hbm, pl.BlockSpec(memory_space=pltpu.SMEM)],
        out_specs=inside,
        scratch_shapes=[
            vmem((4, 256, 16, BOND), BF),
            vmem((4, 256, 16, BOND), BF),
            vmem((4, 256, 16, BOND), BF),
            vmem((64, 256, BOND), BF),
            vmem((32, 256, BOND), BF),
            vmem((16, 256, BOND), BF),
            vmem((4, 64, 4, BOND), BF),
            vmem((16, 256, BOND), BF),
            vmem((64, 256, BOND), BF),
            vmem((8192, 128), F32),
            vmem((8192, 128), F32),
            vmem((2, 2, 256, BOND), BF),
            vmem((2, BOND, BOND), F32),
            vmem((256, BOND), BF),
            vmem((128, BOND), BF),
            vmem((2, BOND, BOND), BF),
            vmem((2, 4, BOND, BOND), BF),
            vmem((2, BOND, BOND), BF),
            vmem((LEGS, 2, 16, BOND), BF),
            vmem((2, 16, BOND), BF),
            vmem((2, 2, BOND, BOND), BF),
            vmem((BOND, BOND), BF),
            vmem((BOND, BOND), BF),
            vmem((LEGS, 16, BOND), BF),
            vmem((16, BOND), BF),
            vmem((2, 2, BOND, BOND), BF),
            *level_sems(2),
            *level_sems(2),
            *level_sems(1),
            dma((5,)),
            dma((2, 1)),
            dma((2, 3)),
            dma((2, 2)),
            dma((2, LEGS)),
            dma((2, LEGS)),
            dma((2, 1)),
            dma((2, 1)),
            dma((2, LEGS)),
            dma((2, LEGS)),
            dma((2, 3)),
            dma((2, 2)),
            dma((2, 1)),
            dma((2, LEGS)),
            vmem((LEGS, 32, BOND), F32),
            vmem((2, 2, 8, BOND), F32),
            vmem((2, 8, BOND), F32),
            vmem((8, BOND), F32),
            vmem((8, BOND), F32),
            vmem((LEGS, 32, BOND), BF),
            vmem((LEGS, 32, BOND), BF),
        ],
        compiler_params=pltpu.CompilerParams(
            collective_id=0, has_side_effects=True, vmem_limit_bytes=67043328
        ),
    )(tensor_low[0], tensor_mid[0], tensor_top[0], child_operators[0], term_choice[0])


def solution(mesh):
    return jax.shard_map(
        on_device,
        mesh=mesh,
        in_specs=(
            P("leaf", None, "leg", None),
            P("leaf", None, "leg", None),
            P("leaf", None, "leg", None),
            P("leaf", None, None, None, None),
            P("leaf", None, None),
        ),
        out_specs=P("leaf", None, "leg", None),
        check_vma=False,
    )
```

```python
import jax
import jax.numpy as jnp
from jax import lax
from jax.experimental import pallas as pl
from jax.experimental.pallas import tpu as pltpu
from jax.sharding import PartitionSpec as P

BF, F32 = jnp.bfloat16, jnp.float32
MESH = pl.DeviceIdType.MESH
BOND = 256
LEGS = 16


def x_near(leg):
    x = leg % 4
    return leg // 4 * 4 + x + 1 - 2 * (x % 2)


def x_far(leg):
    return leg // 4 * 4 + 3 - leg % 4


def y_near(leg):
    y = leg // 4
    return (y + 1 - 2 * (y % 2)) * 4 + leg % 4


def y_far(leg):
    return (3 - leg // 4) * 4 + leg % 4


def pick(core, first, second):
    return first + (second - first) * core


def rows_at(start, size):
    return pl.ds(pl.multiple_of(start, 8), size)


class Level:
    def __init__(self, env, ws, wl, sems, own_rows, own_at, left_bits, gather, spread, halves):
        self.env, self.ws, self.wl = env, ws, wl
        self.a_sem, self.b1_sem, self.bd_sem, self.br_sem, self.loc_sem, self.share_sem = sems
        self.own_rows, self.own_at = own_rows, own_at
        self.n_left = own_rows // 4
        self.left_at = own_at + left_bits * self.n_left
        self.halves, self.part = halves, 16 // halves
        core, leg = env["core"], env["leg"]
        fx, fy = gather
        gx, gy = spread
        self.slot_legs = [leg, fx(leg), fy(leg), fx(fy(leg))]
        self.a1 = pick(core, fx(leg), fy(leg))
        self.a2 = pick(core, fy(leg), fx(leg))
        self.first, self.second = 1 + core, 2 - core
        self.b1 = lambda one: pick(core, gy(one), gx(one))
        self.b2 = lambda one: pick(core, gx(one), gy(one))
        self.leg_of = {"own": leg, "first": self.a1, "second": self.a2, "both": fx(fy(leg))}
        self.slot_of = {"own": 0, "first": self.first, "second": self.second, "both": 3}
        self.pending = []
        self.partner_at = None

    def remote(self, src, dst, sem, index, to):
        return pltpu.make_async_remote_copy(
            src_ref=src,
            dst_ref=dst,
            send_sem=sem.at[(0, *index)],
            recv_sem=sem.at[(1, *index)],
            device_id=to,
            device_id_type=MESH,
        )

    def go(self, copy):
        copy.start()
        self.pending.append(copy)

    def piece(self, slot, h):
        return self.ws.at[
            slot, rows_at(self.left_at, self.n_left), pl.ds(h * self.part, self.part), :
        ]

    def place(self, one, h):
        return self.wl.at[:, rows_at(one * 16 + h * self.part, self.part), :]

    def to(self, one):
        return (self.env["leaf"], one)

    def hop(self, kind, h, arriving):
        src = {"a1": 0, "own": 0, "relay": self.first}[kind]
        dst = {"a1": self.first, "own": self.second, "relay": 3}[kind]
        target = self.a1 if kind == "a1" else self.a2
        index = ({"a1": 0, "own": 1, "relay": 2}[kind], h)
        rows = rows_at(self.own_at, self.own_rows)
        if kind != "a1" and self.partner_at is not None:
            rows = rows_at(self.left_at if arriving else self.partner_at, self.n_left)
        columns = pl.ds(h * self.part, self.part)
        source = self.ws.at[dst if arriving else src, rows, columns, :]
        place = self.ws.at[dst, rows, columns, :]
        return self.remote(source, place, self.a_sem, index, self.to(target))

    def send_hop(self, kind, h):
        self.go(self.hop(kind, h, False))

    def recv_hop(self, kind, h):
        self.hop(kind, h, True).wait_recv()

    def spread(self, name, h):
        slot, one = self.slot_of[name], self.leg_of[name]
        piece, place, leg = self.piece(slot, h), self.place(one, h), self.env["leg"]
        self.go(self.remote(piece, place, self.b1_sem, (slot, h), self.to(self.b1(leg))))
        self.go(self.remote(piece, place, self.bd_sem, (slot, h), self.to(self.b2(leg))))
        copy = pltpu.make_async_copy(piece, place, self.loc_sem.at[slot, h])
        copy.start()
        self.pending.append(copy)

    def relay(self, name, h):
        slot, leg = self.slot_of[name], self.env["leg"]
        place = self.place(self.b1(self.leg_of[name]), h)
        self.remote(place, place, self.b1_sem, (slot, h), self.to(self.b1(leg))).wait_recv()
        self.go(self.remote(place, place, self.br_sem, (slot, h), self.to(self.b2(leg))))

    def arrive(self, name, h):
        slot, leg, one = self.slot_of[name], self.env["leg"], self.leg_of[name]
        place = self.place(self.b2(one), h)
        self.remote(place, place, self.bd_sem, (slot, h), self.to(self.b2(leg))).wait_recv()
        place = self.place(self.b2(self.b1(one)), h)
        self.remote(place, place, self.br_sem, (slot, h), self.to(self.b2(leg))).wait_recv()

    def finish(self):
        for copy in self.pending:
            if copy.is_remote:
                copy.wait_send()

    def finish_local(self):
        for copy in self.pending:
            if not copy.is_remote:
                copy.wait()

    def share(self, name, step, start, size, to):
        slot = self.slot_of[name]
        span = self.ws.at[slot, rows_at(start, size)]
        self.go(self.remote(span, span, self.share_sem, (step, slot), to))

    def shared(self, name, step, start, size, to):
        slot = self.slot_of[name]
        span = self.ws.at[slot, rows_at(start, size)]
        self.remote(span, span, self.share_sem, (step, slot), to).wait_recv()


def transfer(src, dst, sem, index, to):
    return pltpu.make_async_remote_copy(
        src_ref=src,
        dst_ref=dst,
        send_sem=sem.at[(0, *index)],
        recv_sem=sem.at[(1, *index)],
        device_id=to,
        device_id_type=MESH,
    )


def kernel(
    w_low, w_mid, w_top, bank_in, choice, out,
    ws_low, ws_mid, ws_top, wl_low, wl_mid, wl_top, top_parts, by_row_low, by_row_mid, ys_0, ys_1,
    zs, acc, l_cat, r_cat, right_t, bank, sums, inbox, block, ops_a, mate_in, mid_sum, mid_in,
    mid_block, ops_b,
    low_a, low_b1, low_bd, low_br, low_loc, low_share,
    mid_a, mid_b1, mid_bd, mid_br, mid_loc, mid_share,
    top_a, top_b1, top_bd, top_br, top_loc, top_share,
    first_sem, mid_first, top_first, mixed_sem, rs_sem, ag_sem, op_sem,
    mate_sem, rs2_sem, ag2_sem, op2_sem, half_sem, quarter_sem, rs3_sem,
    wide, half_sum, half_in, side_sum, side_in, rows_out, rows_in,
):
    leaf, leg = lax.axis_index("leaf"), lax.axis_index("leg")
    core, z = leaf % 2, leaf // 2
    side = z % 2
    x, y = leg % 4, leg // 4
    far_x, far_y = x // 2, y // 2
    near_x, near_y = (x + far_x) % 2, (y + far_y) % 2
    mate = (leaf + 1 - 2 * core, leg)
    across = (leaf + 2 - 4 * side, leg)
    cross = (leaf + 2 - 4 * side + 1 - 2 * core, leg)
    env = {"leaf": leaf, "leg": leg, "core": core}
    near, far = (x_near, y_near), (x_far, y_far)

    low = Level(
        env, ws_low, wl_low, (low_a, low_b1, low_bd, low_br, low_loc, low_share),
        256, 0, near_x + 2 * near_y, near, far, 2,
    )
    mid = Level(
        env, ws_mid, wl_mid, (mid_a, mid_b1, mid_bd, mid_br, mid_loc, mid_share),
        128, core * 128, near_x + 2 * near_y, near, far, 2,
    )
    top = Level(
        env, ws_top, wl_top, (top_a, top_b1, top_bd, top_br, top_loc, top_share),
        64, core * 128 + side * 64, near_x + 2 * near_y, near, far, 1,
    )
    low.partner_at = 64 * pick(core, near_x + 2 - 2 * near_y, 1 - near_x + 2 * near_y)
    q = side * 2 + core
    mine, theirs = rows_at(core * 8, 8), rows_at(8 - core * 8, 8)
    mid_rows, mate_rows = rows_at(core * 128, 128), rows_at(128 - core * 128, 128)

    own_low = [
        pltpu.make_async_copy(
            w_low.at[:, pl.ds(h * 8, 8), :], ws_low.at[0, :, pl.ds(h * 8, 8), :], first_sem.at[h]
        )
        for h in range(2)
    ]
    own_mid = pltpu.make_async_copy(
        w_mid.at[mid_rows], ws_mid.at[0, mid_rows, mine, :], first_sem.at[2]
    )
    own_top = pltpu.make_async_copy(
        w_top.at[rows_at(top.own_at, 64)], top_parts.at[q], first_sem.at[3]
    )
    own_bank = pltpu.make_async_copy(bank_in, bank, first_sem.at[4])
    for copy in (*own_low, own_bank, own_mid, own_top):
        copy.start()

    barrier = pltpu.get_barrier_semaphore()

    near_by = [(leaf, hop(leg)) for hop in (x_near, x_far, y_near, y_far)]
    for peer in (*near_by, mate, across, cross):
        pl.semaphore_signal(barrier, inc=1, device_id=peer, device_id_type=MESH)
    pl.semaphore_wait(barrier, len(near_by) + 3)

    for h in range(2):
        own_low[h].wait()
        low.send_hop("a1", h)
        low.send_hop("own", h)
    mid_out = transfer(
        w_mid.at[mate_rows], ws_mid.at[0, mate_rows, mine, :], mid_first, (0,), mate
    )
    mid_out.start()
    quarters = [
        ((1 - core) * 128 + side * 64, side * 2 + 1 - core, mate),
        (core * 128 + (1 - side) * 64, (1 - side) * 2 + core, across),
        ((1 - core) * 128 + (1 - side) * 64, (1 - side) * 2 + 1 - core, cross),
    ]
    top_sends = []
    for n, (start, _, peer) in enumerate(quarters):
        copy = transfer(w_top.at[rows_at(start, 64)], top_parts.at[q], top_first, (n,), peer)
        copy.start()
        top_sends.append(copy)
    for h in range(2):
        low.spread("own", h)

    def load_left(read, n_left, at, start=0):
        for t in range(2):
            l_cat[start + t * n_left : start + (t + 1) * n_left] = read(t, rows_at(at, n_left))

    def load_right(legs):
        for t in range(2):
            for slot, one in enumerate(legs):
                start = t * 64 + slot * 16
                r_cat[start : start + 16] = right_t[t, rows_at(one * 16, 16), :]

    def mix_rows(slot, s, rows, n_left):
        mixed = jnp.dot(l_cat[: 2 * n_left], rows, preferred_element_type=F32)
        span = pl.ds(slot * 16 + s, 2 * n_left, stride=64)
        ys_0[span, :] = mixed[:, :128]
        ys_1[span, :] = mixed[:, 128:]

    def mixed_at(turn, arriving):
        return by_row_mid.at[pl.ds(32 + turn * 16, 16), pl.ds(128 * arriving, 128), :]

    def mixed_copy(turn, arriving):
        source = mixed_at(turn, 1 if arriving else 0)
        return transfer(source, mixed_at(turn, 1), mixed_sem, (turn,), (leaf, low.a2))

    def mix_low(turn, name):
        slot = low.slot_of[name]

        @pl.loop(0, 16, unroll=2)
        def _(n):
            by_row_low[:, pl.ds(n * 16, 16), :] = jnp.swapaxes(ws_low[slot, pl.ds(n * 16, 16)], 0, 1)

        @pl.loop(0, 16, unroll=4)
        def _(s):
            mixed = jnp.dot(l_cat[...], by_row_low[s], preferred_element_type=F32)
            span = pl.ds(slot * 16 + s, 128, stride=64)
            ys_0[span, :] = mixed[:128, :128]
            ys_1[span, :] = mixed[:128, 128:]
            by_row_mid[32 + turn * 16 + s, :128, :] = mixed[128:].astype(BF)

    def take_low(turn, name):
        slot = low.slot_of[name]
        mixed_copy(turn, True).wait_recv()

        @pl.loop(0, 16, unroll=4)
        def _(s):
            mixed = by_row_mid[32 + turn * 16 + s, 128:, :].astype(F32)
            span = pl.ds(slot * 16 + s, 128, stride=64)
            ys_0[span, :] = mixed[:, :128]
            ys_1[span, :] = mixed[:, 128:]

    def turn_mid(name, half):
        slot = mid.slot_of[name]

        @pl.loop(0, 8, unroll=2)
        def _(n):
            rows = rows_at(half * 128 + n * 16, 16)
            by_row_mid[pl.ds(slot * 16, 16), rows, :] = jnp.swapaxes(ws_mid[slot, rows], 0, 1)

    def mix_mid():
        @pl.loop(0, 64, unroll=8)
        def _(s):
            mix_rows(0, s, by_row_mid[s], mid.n_left)

    def turn_top(name, half):
        slot = top.slot_of[name]

        @pl.loop(0, 8, unroll=2)
        def _(n):
            at = half * 8 + n
            turned = jnp.swapaxes(ws_top[slot, rows_at(at * 16, 16)], 0, 1)
            for s in range(16):
                ws_low[slot, s * 16 + at] = turned[s]

    def mix_top(name):
        slot = top.slot_of[name]

        @pl.loop(0, 16, unroll=8)
        def _(s):
            rows = ws_low[slot, pl.ds(s * 16, 16)]
            mix_rows(slot, s, rows.reshape(256, BOND), top.n_left)

    def contract(level):
        acc[...] = jnp.zeros_like(acc)
        n_left = level.n_left

        @pl.loop(0, n_left // 4, unroll=4)
        def _(n):
            for k in range(4):
                turned = jnp.dot(
                    r_cat[...], level.wl[n * 4 + k], preferred_element_type=F32
                ).astype(BF)
                for t in range(2):
                    zs[n % 2, t, k * 64 : (k + 1) * 64] = turned[t * 64 : (t + 1) * 64]
            for t in range(2):
                span = rows_at((t * n_left + n * 4) * 64, 256)
                rows = jnp.concatenate([ys_0[span, :], ys_1[span, :]], axis=1).astype(BF)
                acc[t] += lax.dot_general(
                    zs[n % 2, t], rows, (((0,), (0,)), ((), ())), preferred_element_type=F32
                )

    def ring_start(src_of, dst_of, sem):
        @pl.loop(1, LEGS)
        def _(d):
            one = (leg + d) % LEGS
            transfer(src_of(one), dst_of(d), sem, (d,), (leaf, one)).start()

    def ring_recv(dst_of, sem):
        @pl.loop(1, LEGS)
        def _(d):
            ref = dst_of(d)
            transfer(ref, ref, sem, (d,), (leaf, (leg + d) % LEGS)).wait_recv()

    def ring_sent(src_of, sem):
        @pl.loop(1, LEGS)
        def _(d):
            one = (leg + d) % LEGS
            ref = src_of(one)
            transfer(ref, ref, sem, (d,), (leaf, one)).wait_send()

    def mid_share(name):
        mid.share(name, 0, mid.own_at, 128, mate)

    def mid_shared(name):
        mid.shared(name, 0, 128 - core * 128, 128, mate)

    def top_shared(name):
        top.shared(name, 1, 128 - core * 128, 128, mate)

    def top_across(name):
        top.shared(name, 0, core * 128 + (1 - side) * 64, 64, across)
        top.share(name, 1, core * 128, 128, mate)

    own_top.wait()
    for n, (_, part, peer) in enumerate(quarters):
        transfer(
            w_top.at[rows_at(top.own_at, 64)], top_parts.at[part], top_first, (n,), peer
        ).wait_recv()

    @pl.loop(0, 4)
    def _(n):
        for part in range(4):
            wide[:, part * 4 : part * 4 + 4, :] = top_parts[part, pl.ds(n * 16, 16), :, :].astype(
                F32
            )
        ws_top[0, rows_at(top.own_at + n * 16, 16), :, :] = wide[:, :16, :].astype(BF)

    own_bank.wait()
    for start, at in ((0, low.left_at), (128, low.partner_at)):
        load_left(lambda t, rows: bank[0, choice[t, 0], rows, :], 64, at, start)
    for t in range(2):
        right_t[t] = bank[1, choice[t, 1]].T
    load_right(low.slot_legs)
    own_mid.wait()
    transfer(
        w_mid.at[mid_rows], ws_mid.at[0, mid_rows, theirs, :], mid_first, (0,), mate
    ).wait_recv()
    mid_share("own")
    top.share("own", 0, top.own_at, 64, across)
    mix_low(0, "own")
    for h in range(2):
        low.recv_hop("own", h)
        low.spread("second", h)
    low.recv_hop("a1", 0)
    low.send_hop("relay", 0)
    mixed_copy(0, False).start()
    low.spread("first", 0)
    for h in range(2):
        low.relay("own", h)
    for h in range(2):
        low.relay("second", h)
    low.recv_hop("a1", 1)
    low.send_hop("relay", 1)
    low.spread("first", 1)
    mix_low(1, "first")
    mixed_copy(1, False).start()
    low.recv_hop("relay", 0)
    low.spread("both", 0)
    low.relay("first", 0)
    low.recv_hop("relay", 1)
    low.spread("both", 1)
    for h in range(2):
        mid.send_hop("a1", h)
    low.relay("both", 0)
    low.relay("first", 1)
    take_low(0, "second")
    low.relay("both", 1)
    take_low(1, "both")
    for name in ("own", "first", "both", "second"):
        for h in range(2):
            low.arrive(name, h)
    mid.recv_hop("a1", 0)
    mid.send_hop("relay", 0)
    mid.send_hop("own", 0)
    for h in range(2):
        mid.spread("own", h)
    mid.spread("first", 0)
    top_across("own")
    for turn in range(2):
        mixed_copy(turn, False).wait_send()
    low.finish_local()
    contract(low)

    sums[...] = acc[...].astype(BF)
    ring_start(lambda one: sums.at[:, rows_at(one * 16, 16), :], lambda d: inbox.at[d], rs_sem)
    mid.recv_hop("a1", 1)
    mid.send_hop("relay", 1)
    mid.send_hop("own", 1)
    mid.spread("first", 1)
    mid_share("first")
    top.send_hop("a1", 0)
    for h in range(2):
        mid.relay("own", h)
    mid.recv_hop("relay", 0)
    mid.spread("both", 0)
    turn_mid("own", core)
    mid_shared("own")
    turn_mid("own", 1 - core)
    mid.recv_hop("own", 0)
    mid.spread("second", 0)
    mid.relay("first", 0)
    turn_mid("first", core)
    ring_recv(lambda d: inbox.at[d], rs_sem)
    total = acc[:, rows_at(leg * 16, 16), :]
    for d in range(1, LEGS):
        total = total + inbox[d].astype(F32)
    block[...] = total.astype(BF)
    ops_a[core, :, rows_at(leg * 16, 16), :] = total.astype(BF)
    ring_start(
        lambda one: block, lambda d: ops_a.at[core, :, rows_at(leg * 16, 16), :], ag_sem
    )
    top.recv_hop("a1", 0)
    top.send_hop("relay", 0)
    top.share("first", 0, top.own_at, 64, across)
    mid.relay("first", 1)
    mid_shared("second")
    turn_mid("second", 1 - core)
    mid.recv_hop("relay", 1)
    mid.spread("both", 1)
    mid_share("both")
    mid.recv_hop("own", 1)
    mid.spread("second", 1)
    mid_share("second")
    top.send_hop("own", 0)
    mid.relay("both", 0)
    mid.relay("second", 0)
    turn_mid("both", core)
    turn_mid("second", core)
    mid.relay("both", 1)
    ring_recv(
        lambda d: ops_a.at[core, :, rows_at((leg - d + LEGS) % LEGS * 16, 16), :], ag_sem
    )
    op_send = transfer(ops_a.at[core], ops_a.at[core], op_sem, (0,), mate)
    op_send.start()
    mid_shared("both")
    turn_mid("both", 1 - core)
    mid_shared("first")
    turn_mid("first", 1 - core)
    top_across("first")
    low.finish()
    transfer(ops_a.at[1 - core], ops_a.at[1 - core], op_sem, (0,), mate).wait_recv()

    load_left(lambda t, rows: ops_a[0, t, rows, :], mid.n_left, mid.left_at)
    for t in range(2):
        right_t[t] = ops_a[1, t].T
    load_right(mid.slot_legs)
    mix_mid()
    mid.relay("second", 1)
    top.recv_hop("relay", 0)
    top.share("both", 0, top.own_at, 64, across)
    for name in ("own", "first"):
        top.spread(name, 0)
    top.recv_hop("own", 0)
    top.share("second", 0, top.own_at, 64, across)
    for name in ("both", "second"):
        top.spread(name, 0)
    top_shared("own")
    for half in range(2):
        turn_top("own", half)
    for name in ("own", "first", "both", "second"):
        for h in range(2):
            mid.arrive(name, h)
    mid.finish_local()
    contract(mid)

    ring_sent(lambda one: sums.at[:, rows_at(one * 16, 16), :], rs_sem)
    sums[...] = acc[...].astype(BF)
    mate_send = transfer(sums.at[1 - core], mate_in, mate_sem, (0,), mate)
    mate_send.start()
    transfer(mate_in, mate_in, mate_sem, (0,), mate).wait_recv()
    mid_sum[...] = (acc[core] + mate_in[...].astype(F32)).astype(BF)
    ring_start(lambda one: mid_sum.at[rows_at(one * 16, 16), :], lambda d: mid_in.at[d], rs2_sem)
    own_rows = rows_at(leg * 16, 16)
    total = acc[core, own_rows, :] + mate_in[own_rows, :].astype(F32)
    top_shared("second")
    turn_top("second", 1 - core)
    turn_top("first", core)
    ring_recv(lambda d: mid_in.at[d], rs2_sem)
    for d in range(1, LEGS):
        total = total + mid_in[d].astype(F32)
    mid_block[...] = total.astype(BF)
    ops_b[side, core, own_rows, :] = total.astype(BF)
    ring_start(lambda one: mid_block, lambda d: ops_b.at[side, core, own_rows, :], ag2_sem)
    top.relay("own", 0)
    top.relay("first", 0)
    top_across("both")
    turn_top("both", core)
    ring_recv(
        lambda d: ops_b.at[side, core, rows_at((leg - d + LEGS) % LEGS * 16, 16), :], ag2_sem
    )
    ours = ops_b.at[side, core]
    op2_sends = [
        transfer(ours, ours, op2_sem, (0,), mate),
        transfer(ours, ours, op2_sem, (1,), across),
    ]
    for copy in op2_sends:
        copy.start()
    top_shared("both")
    turn_top("both", 1 - core)
    top_across("second")
    turn_top("second", core)
    top.relay("both", 0)
    top.relay("second", 0)
    other = ops_b.at[1 - side, core]
    transfer(other, other, op2_sem, (1,), across).wait_recv()
    op2_sends.append(transfer(other, other, op2_sem, (2,), mate))
    op2_sends[-1].start()
    for n, ref in ((0, ops_b.at[side, 1 - core]), (2, ops_b.at[1 - side, 1 - core])):
        transfer(ref, ref, op2_sem, (n,), mate).wait_recv()

    load_left(lambda t, rows: ops_b[0, t, rows, :], top.n_left, top.left_at)
    for t in range(2):
        right_t[t] = ops_b[1, t].T
    load_right(top.slot_legs)
    mix_top("own")
    mix_top("both")
    top_shared("first")
    turn_top("first", 1 - core)
    mix_top("first")
    mix_top("second")
    for name in ("own", "first", "both", "second"):
        top.arrive(name, 0)
    top.finish_local()
    contract(top)

    for one in range(LEGS):
        for t in range(2):
            for part in range(4):
                at = part * 64 + one * 4
                wide[one, part * 8 + t * 4 : part * 8 + t * 4 + 4, :] = acc[t, at : at + 4, :]
    rows_out[...] = wide[...].astype(BF)
    ring_start(lambda one: rows_out.at[one], lambda d: rows_in.at[d], rs3_sem)
    total = wide[leg]
    ring_recv(lambda d: rows_in.at[d], rs3_sem)
    for d in range(1, LEGS):
        total = total + rows_in[d].astype(F32)
    half_sum[...] = total.reshape(2, 2, 8, BOND)
    half_sends = []
    for n in range(2):
        copy = transfer(half_sum.at[n, 1 - core], half_in.at[n], half_sem, (n,), mate)
        copy.start()
        half_sends.append(copy)
    for n in range(2):
        transfer(half_in.at[n], half_in.at[n], half_sem, (n,), mate).wait_recv()
    side_sum[...] = half_sum[1 - side, core] + half_in[1 - side]
    side_send = transfer(side_sum, side_in, quarter_sem, (0,), across)
    side_send.start()
    total = half_sum[side, core] + half_in[side]
    transfer(side_in, side_in, quarter_sem, (0,), across).wait_recv()
    total = total + side_in[...]
    for t in range(2):
        out[0, t] = total[t * 4 : t * 4 + 4]

    for level in (mid, top):
        level.finish()
    mid_out.wait_send()
    for copy in (*top_sends, op_send, mate_send, *op2_sends, *half_sends, side_send):
        copy.wait_send()
    ring_sent(lambda one: block, ag_sem)
    ring_sent(lambda one: mid_sum.at[rows_at(one * 16, 16), :], rs2_sem)
    ring_sent(lambda one: mid_block, ag2_sem)
    ring_sent(lambda one: rows_out.at[one], rs3_sem)


def on_device(tensor_low, tensor_mid, tensor_top, child_operators, term_choice):
    dma, vmem = pltpu.SemaphoreType.DMA, pltpu.VMEM

    def level_sems(halves):
        return [
            dma((2, 3, halves)),
            dma((2, 4, halves)),
            dma((2, 4, halves)),
            dma((2, 4, halves)),
            dma((4, halves)),
            dma((2, 2, 4)),
        ]

    hbm = pl.BlockSpec(memory_space=pl.ANY)
    inside = pl.BlockSpec(memory_space=pltpu.VMEM)
    return pl.pallas_call(
        kernel,
        out_shape=jax.ShapeDtypeStruct((1, 2, 4, BOND), F32),
        in_specs=[hbm, hbm, hbm, hbm, pl.BlockSpec(memory_space=pltpu.SMEM)],
        out_specs=inside,
        scratch_shapes=[
            vmem((4, 256, 16, BOND), BF),
            vmem((4, 256, 16, BOND), BF),
            vmem((4, 256, 16, BOND), BF),
            vmem((64, 256, BOND), BF),
            vmem((32, 256, BOND), BF),
            vmem((16, 256, BOND), BF),
            vmem((4, 64, 4, BOND), BF),
            vmem((16, 256, BOND), BF),
            vmem((64, 256, BOND), BF),
            vmem((8192, 128), F32),
            vmem((8192, 128), F32),
            vmem((2, 2, 256, BOND), BF),
            vmem((2, BOND, BOND), F32),
            vmem((256, BOND), BF),
            vmem((128, BOND), BF),
            vmem((2, BOND, BOND), BF),
            vmem((2, 4, BOND, BOND), BF),
            vmem((2, BOND, BOND), BF),
            vmem((LEGS, 2, 16, BOND), BF),
            vmem((2, 16, BOND), BF),
            vmem((2, 2, BOND, BOND), BF),
            vmem((BOND, BOND), BF),
            vmem((BOND, BOND), BF),
            vmem((LEGS, 16, BOND), BF),
            vmem((16, BOND), BF),
            vmem((2, 2, BOND, BOND), BF),
            *level_sems(2),
            *level_sems(2),
            *level_sems(1),
            dma((5,)),
            dma((2, 1)),
            dma((2, 3)),
            dma((2, 2)),
            dma((2, LEGS)),
            dma((2, LEGS)),
            dma((2, 1)),
            dma((2, 1)),
            dma((2, LEGS)),
            dma((2, LEGS)),
            dma((2, 3)),
            dma((2, 2)),
            dma((2, 1)),
            dma((2, LEGS)),
            vmem((LEGS, 32, BOND), F32),
            vmem((2, 2, 8, BOND), F32),
            vmem((2, 8, BOND), F32),
            vmem((8, BOND), F32),
            vmem((8, BOND), F32),
            vmem((LEGS, 32, BOND), BF),
            vmem((LEGS, 32, BOND), BF),
        ],
        compiler_params=pltpu.CompilerParams(
            collective_id=0, has_side_effects=True, vmem_limit_bytes=67043328
        ),
    )(tensor_low[0], tensor_mid[0], tensor_top[0], child_operators[0], term_choice[0])


def solution(mesh):
    return jax.shard_map(
        on_device,
        mesh=mesh,
        in_specs=(
            P("leaf", None, "leg", None),
            P("leaf", None, "leg", None),
            P("leaf", None, "leg", None),
            P("leaf", None, None, None, None),
            P("leaf", None, None),
        ),
        out_specs=P("leaf", None, "leg", None),
        check_vma=False,
    )
```
